256 devices in a mesh: chan: 8 (over z), tm: 32 (over y, x, core).
Axes of the slice: x: 4, y: 4, z: 8, core: 2. Of those that a mesh axis runs over, the one named last changes fastest.
Arguments:
- symbols: int32 [64, 262144], P('chan', 'tm'), may hold values from 0 to 63
- incidence: int32 [256, 6], P('chan'), may hold values from 0 to 63, as said below
- delays: int32 [256, 6], P('chan'), may hold values from 0 to 63
- gains: float32 [2, 256, 6], P(None, 'chan'), may hold values from -4 to 4
- echoes: bfloat16 [2, 256, 262144], P(None, 'chan', 'tm'), may hold values from -6 to 6
Outputs:
- cancelled: bfloat16 [2, 256, 262144], P(None, 'chan', 'tm')
- weights: float32 [2, 256, 384], P(None, 'chan')
The draws below stay inside these ranges and needn't reach their ends.
Inputs may be any that keep to these rules, and one draw needn't show every extreme that they name: `incidence`: row r names 6 distinct illuminators, all owned by chan index c = r // 32 or the next index c + 1 taken cyclically: ids from c * 8 to (c + 2) * 8 - 1, modulo 64.
All inputs are finite; a program needn't handle non-finite values.
Results may differ from the reference program's by a relative error of at most 0.024.
Values may be sent and summed in bfloat16 or wider, within the bound.
No kernel may reach another device: no remote copies, remote signals or barrier semaphores. Data moves between devices by JAX's collectives and lax.ppermute only.
A program may use at most 64 MiB of HBM per device.

```python
import math
import jax
import jax.numpy as jnp
from jax import lax

FOURIER_LENGTH = 8192
ACTIVE = 6817
DELAYS = 64
PER_RECV = 6
I_DEV = 8
R_DEV = 32
ILLUM = 64
RECV = 256
SAMPLES = 262144


def draw_incidence(key, part):
    owner_base = jnp.arange(RECV, dtype=jnp.int32) // R_DEV
    row_keys = jax.random.split(jax.random.fold_in(key, 11), RECV)
    chosen_slots = jax.vmap(lambda row_key: jax.random.permutation(row_key, 2 * I_DEV)[:PER_RECV])(row_keys).astype(jnp.int32)
    owner_chan = (owner_base[:, None] + chosen_slots // I_DEV) % (ILLUM // I_DEV)
    return (owner_chan * I_DEV + chosen_slots % I_DEV).astype(jnp.int32)


def touch_ends(entries, key, smallest, high):
    longest = entries.shape.index(max(entries.shape))
    spots = []
    for shift in (0, 1):
        where = [jax.random.randint(jax.random.fold_in(key, axis), (), 0, length) for axis, length in enumerate(entries.shape)]
        where[longest] = (where[longest] + shift) % entries.shape[longest]
        spots.append(tuple(where))
    return entries.at[spots[0]].set(smallest).at[spots[1]].set(high)


def levels(stream_key, dims, cuts, smallest, top_value):
    level = 1.0
    for position, parts in cuts:
        draws = jax.random.uniform(jax.random.fold_in(jax.random.fold_in(stream_key, 6), position), (parts,), jnp.float32, smallest / len(cuts), top_value / len(cuts))
        level = level * jnp.repeat(jnp.exp(draws), dims[position] // parts).reshape((-1,) + (1,) * (len(dims) - 1 - position))
    return level


def normal_values(stream_key, extent, scale, reach, cuts=(), kind=jnp.bfloat16):
    values = jax.random.normal(stream_key, extent, jnp.float32) * scale
    if len(cuts) > 0:
        values = levels(stream_key, extent, cuts, -0.22, 0.18) * values
    return jnp.clip(values, min=-reach, max=reach).astype(kind)


def setup_inputs(seed: int = 0) -> dict:
    streams_of = jax.random.split(jax.random.key(seed), 6)
    symbols = touch_ends(jax.random.randint(streams_of[0], (ILLUM, SAMPLES), 0, 64), jax.random.fold_in(streams_of[0], 1), 0, 63).astype(jnp.int32)
    incidence = draw_incidence(jax.random.fold_in(streams_of[5], 71), 0)
    delays = touch_ends(jax.random.randint(streams_of[2], (RECV, PER_RECV), 0, DELAYS), jax.random.fold_in(streams_of[2], 1), 0, DELAYS - 1).astype(jnp.int32)
    gains = normal_values(streams_of[3], (2, RECV, PER_RECV), 1.0, 4.0, ((1, 8),), jnp.float32)
    echoes = normal_values(streams_of[4], (2, RECV, SAMPLES), 1.0, 6.0, ((1, 8), (2, 32)))
    return {"symbols": symbols, "incidence": incidence, "delays": delays, "gains": gains, "echoes": echoes}


loading = 0.1

def reference(symbols, incidence, delays, gains, echoes):
    emitter_number = symbols.shape[0]
    samples = symbols.shape[1]
    processor_portions = samples // FOURIER_LENGTH
    blocks = samples // DELAYS
    key_len = PER_RECV * DELAYS
    inphase_amplitude = (2 * (symbols % 8) - 7).astype(jnp.float32) / math.sqrt(42.0)
    quadrature_amplitude = (2 * (symbols // 8) - 7).astype(jnp.float32) / math.sqrt(42.0)
    subcarrier = jnp.arange(FOURIER_LENGTH, dtype=jnp.int32) - FOURIER_LENGTH // 2
    occupied_tones = (jnp.abs(subcarrier) <= (ACTIVE - 1) // 2).astype(jnp.float32)
    tone_symbols = (inphase_amplitude + 1j * quadrature_amplitude).reshape(emitter_number, processor_portions, FOURIER_LENGTH) * occupied_tones
    waveform_samples = jnp.fft.ifft(tone_symbols, axis=-1) * FOURIER_LENGTH
    alternate = (1 - 2 * (jnp.arange(FOURIER_LENGTH, dtype=jnp.int32) % 2)).astype(jnp.float32) / math.sqrt(ACTIVE)
    waveform_samples = (waveform_samples * alternate).reshape(emitter_number, samples)
    ref_re = jnp.real(waveform_samples).astype(jnp.bfloat16)
    ref_im = jnp.imag(waveform_samples).astype(jnp.bfloat16)
    padded = jnp.pad(jnp.stack([ref_re, ref_im], axis=1), ((0, 0), (0, 0), (DELAYS, 0)))
    pieces = padded.astype(jnp.float32).reshape(emitter_number, 2, blocks + 1, DELAYS)
    frames = jnp.concatenate([pieces[:, :, :-1], pieces[:, :, 1:]], axis=3)
    frame_freq = jnp.fft.fft(frames[:, 0] + 1j * frames[:, 1], axis=-1)
    current = pieces[:, 0, 1:] + 1j * pieces[:, 1, 1:]
    current = jnp.pad(current, ((0, 0), (0, 0), (0, DELAYS)))
    current_freq = jnp.fft.fft(current, axis=-1)
    pair_freq = jnp.einsum('iqf,jqf->fij', jnp.conj(frame_freq), current_freq)
    lag_index = DELAYS - jnp.arange(DELAYS, dtype=jnp.int32)
    corr = (jnp.fft.fft(pair_freq, axis=0) / (2 * DELAYS))[lag_index] / samples
    corr_re = jnp.transpose(jnp.real(corr), (1, 2, 0))
    corr_im = jnp.transpose(jnp.imag(corr), (1, 2, 0))
    lag_diff = jnp.arange(DELAYS, dtype=jnp.int32)[:, None] - jnp.arange(DELAYS, dtype=jnp.int32)[None, :]
    below_diag = lag_diff >= 0
    forward_lag = jnp.clip(lag_diff, 0, DELAYS - 1)
    backward_lag = jnp.clip(-lag_diff, 0, DELAYS - 1)
    identity = jnp.eye(key_len, dtype=jnp.float32)

    def per_receiver(inputs):
        chosen, lag_values, gain, echo = inputs
        rows = padded[chosen]
        shifted = jax.vmap(lambda ref_row, lag_value: lax.dynamic_slice_in_dim(ref_row, DELAYS - lag_value, samples, 1))(rows, lag_values).astype(jnp.float32)
        direct_re = lax.optimization_barrier(jnp.sum(gain[0][:, None] * shifted[:, 0] - gain[1][:, None] * shifted[:, 1], axis=0))
        direct_im = lax.optimization_barrier(jnp.sum(gain[0][:, None] * shifted[:, 1] + gain[1][:, None] * shifted[:, 0], axis=0))
        received = jnp.stack([echo[0].astype(jnp.float32) + direct_re, echo[1].astype(jnp.float32) + direct_im]).astype(jnp.bfloat16)
        signal = received.astype(jnp.float32).reshape(2, blocks, DELAYS)
        signal_c = jnp.pad(signal[0] + 1j * signal[1], ((0, 0), (0, DELAYS)))
        signal_freq = jnp.fft.fft(signal_c, axis=-1)
        chosen_freq = frame_freq[chosen]
        cross_freq = jnp.einsum('kqf,qf->fk', jnp.conj(chosen_freq), signal_freq)
        cross = (jnp.fft.fft(cross_freq, axis=0) / (2 * DELAYS))[lag_index] / samples
        cross_re = jnp.real(cross).T.reshape(key_len)
        cross_im = jnp.imag(cross).T.reshape(key_len)
        sub_re = corr_re[chosen][:, chosen]
        sub_im = corr_im[chosen][:, chosen]
        swap_re = jnp.transpose(sub_re, (1, 0, 2))
        swap_im = jnp.transpose(sub_im, (1, 0, 2))
        gram_re = jnp.where(below_diag, sub_re[:, :, forward_lag], swap_re[:, :, backward_lag])
        gram_im = jnp.where(below_diag, sub_im[:, :, forward_lag], -swap_im[:, :, backward_lag])
        gram_re = jnp.transpose(gram_re, (0, 2, 1, 3)).reshape(key_len, key_len) + loading * identity
        gram_im = jnp.transpose(gram_im, (0, 2, 1, 3)).reshape(key_len, key_len)
        system = jnp.concatenate([jnp.concatenate([gram_re, -gram_im], axis=1), jnp.concatenate([gram_im, gram_re], axis=1)], axis=0)
        factor = jnp.linalg.cholesky(system)
        solved = jax.scipy.linalg.cho_solve((factor, True), jnp.concatenate([cross_re, cross_im]))
        rounded = lax.optimization_barrier(solved.astype(jnp.bfloat16)).astype(jnp.float32)
        tap_c = rounded[:key_len].reshape(PER_RECV, DELAYS) + 1j * rounded[key_len:].reshape(PER_RECV, DELAYS)
        tap_freq = jnp.fft.fft(jnp.pad(tap_c, ((0, 0), (0, DELAYS))), axis=-1)
        proj_freq = jnp.einsum('kqf,kf->qf', chosen_freq, tap_freq)
        projected = jnp.fft.ifft(proj_freq, axis=-1)[:, DELAYS:]
        result = jnp.stack([signal[0].reshape(samples) - jnp.real(projected).reshape(samples), signal[1].reshape(samples) - jnp.imag(projected).reshape(samples)]).astype(jnp.bfloat16)
        return (result, jnp.stack([solved[:key_len], solved[key_len:]]))
    cancelled, weights = lax.map(per_receiver, (incidence, delays, jnp.transpose(gains, (1, 0, 2)), jnp.transpose(echoes, (1, 0, 2))))
    return (jnp.transpose(cancelled, (1, 0, 2)), jnp.transpose(weights, (1, 0, 2)))
```

```python
import math

import jax
import jax.numpy as jnp
from jax import lax
from jax.experimental import pallas as pl
from jax.experimental.pallas import tpu as pltpu
from jax.sharding import PartitionSpec as P

ACTIVE = 6817
DELAYS = 64
PER_RECV = 6
LANES = 128
FINE = 16
COARSE = DELAYS // FINE


loading = 0.1
HIGHEST = lax.Precision.HIGHEST


def passed_along(array, axis, by):
    peers = lax.axis_size(axis)
    return lax.ppermute(array, axis, [(i, (i + by) % peers) for i in range(peers)])


def from_behind(block, axis, distance):
    devices = range(lax.axis_size(axis))
    route = [(i - distance, i) for i in devices if i - distance in devices]
    return lax.ppermute(block, axis, route)


def rotation_angle_grid(row_count, col_count, period):
    product = (
        jnp.arange(row_count, dtype=jnp.int32)[:, None]
        * jnp.arange(col_count, dtype=jnp.int32)[None, :]
    )
    phases = (product % period).astype(jnp.float32) * (2.0 * math.pi / period)
    return (jnp.cos(phases), jnp.sin(phases))


def complex_multiply_result(pattern, left_pair, right_pair):
    real_part = jnp.einsum(pattern, left_pair[0], right_pair[0], precision=HIGHEST) - jnp.einsum(
        pattern, left_pair[1], right_pair[1], precision=HIGHEST
    )
    imag_part = jnp.einsum(pattern, left_pair[0], right_pair[1], precision=HIGHEST) + jnp.einsum(
        pattern, left_pair[1], right_pair[0], precision=HIGHEST
    )
    return (real_part, imag_part)


def remodulate(symbols):
    emitter_number, length = symbols.shape
    column_entries = 128
    increment_spacing = length // column_entries
    inphase_amplitude = (2 * (symbols % 8) - 7).astype(jnp.float32) / math.sqrt(42.0)
    quadrature_amplitude = (2 * (symbols // 8) - 7).astype(jnp.float32) / math.sqrt(42.0)
    subcarrier = jnp.arange(length, dtype=jnp.int32) - length // 2
    occupied_tones = (jnp.abs(subcarrier) <= (ACTIVE - 1) // 2).astype(jnp.float32)
    tone_symbols = (
        (inphase_amplitude * occupied_tones).reshape(
            emitter_number, increment_spacing, column_entries
        ),
        (quadrature_amplitude * occupied_tones).reshape(
            emitter_number, increment_spacing, column_entries
        ),
    )
    partial_result = complex_multiply_result(
        "mb,nbd->nmd",
        rotation_angle_grid(increment_spacing, increment_spacing, increment_spacing),
        tone_symbols,
    )
    twiddle = rotation_angle_grid(increment_spacing, column_entries, length)
    partial_result = (
        partial_result[0] * twiddle[0] - partial_result[1] * twiddle[1],
        partial_result[0] * twiddle[1] + partial_result[1] * twiddle[0],
    )
    frequency_spectrum = complex_multiply_result(
        "pho,oj->phj",
        partial_result,
        rotation_angle_grid(column_entries, column_entries, column_entries),
    )
    alternate = (1 - 2 * (jnp.arange(length, dtype=jnp.int32) % 2)).astype(jnp.float32) / math.sqrt(
        ACTIVE
    )
    real_part = (
        jnp.swapaxes(frequency_spectrum[0], 1, 2).reshape(emitter_number, length) * alternate
    )
    imag_part = (
        jnp.swapaxes(frequency_spectrum[1], 1, 2).reshape(emitter_number, length) * alternate
    )
    return jnp.stack([real_part, imag_part], axis=0).astype(jnp.bfloat16)


def iota(shape, axis):
    return lax.broadcasted_iota(jnp.int32, shape, axis)


def build_shifted(ref_ref, shifted_ref):
    rows, width = ref_ref.shape
    piece = 640

    def one_piece(step, _):
        start = pl.multiple_of(step * piece, LANES)
        before = pl.multiple_of(jnp.maximum(start - LANES, 0), LANES)
        first = ref_ref[:, pl.ds(before, LANES)].astype(jnp.float32)
        body = ref_ref[:, pl.ds(start, piece)].astype(jnp.float32)
        source = jnp.concatenate([first, body], axis=1)
        for row in range(rows):
            spread = jnp.broadcast_to(source[row : row + 1, :], (FINE, LANES + piece))
            rolled = pltpu.roll(spread, 0, 1, stride=1, stride_axis=0)
            shifted_ref[row * FINE : (row + 1) * FINE, pl.ds(start, piece)] = rolled[
                :, LANES:
            ].astype(jnp.bfloat16)
        return 0

    lax.fori_loop(0, width // piece, one_piece, 0)


def lay_taps(tap_rows, slot_rows, receivers):
    cols = 32 * FINE
    lane = iota((LANES, cols), 1)
    source = iota((LANES, cols), 0)
    fine = lane & (FINE - 1)
    in_part = (lane >> 7) & 1
    col_slot = ((iota((1, cols), 1) >> 8) << 3) + ((iota((1, cols), 1) >> 4) & 7)
    blocks = []
    for coarse in range(COARSE):
        for out_part in range(2):
            part = in_part ^ out_part
            sign = jnp.where((in_part == 1) & (out_part == 0), -1.0, 1.0)
            spread = jnp.where(source == part * DELAYS + coarse * FINE + fine, sign, 0.0)
            wide = jnp.dot(
                tap_rows, spread.astype(jnp.bfloat16), preferred_element_type=jnp.float32
            )
            total = jnp.zeros((receivers, cols), jnp.float32)
            for k in range(PER_RECV):
                rows = slice(k * receivers, (k + 1) * receivers)
                total = total + jnp.where(
                    slot_rows[rows, 0:1] == col_slot, wide[rows, :], 0.0
                )
            blocks.append(total)
    return jnp.concatenate(blocks, axis=0).astype(jnp.bfloat16)


def coarse_sum(spread):
    rows = spread.shape[0] // COARSE
    total = spread[:rows, LANES:]
    for coarse in range(1, COARSE):
        total = total + pltpu.roll(spread[coarse * rows : (coarse + 1) * rows], coarse * FINE, 1)[:, LANES:]
    return total


def receive_kernel(
    slot_ref, tap_high_ref, tap_low_ref, slot_rows_ref, refs_ref, echo_ref,
    received_ref, cross_ref, corr_ref, shifted, taps_high, taps_low, signal, outer, tidy, picked,
):
    receivers = echo_ref.shape[0] // 2
    length = echo_ref.shape[1]
    width = length + LANES
    rows = 2 * receivers + 32
    build_shifted(refs_ref, shifted)
    taps_high[...] = lay_taps(tap_high_ref[...], slot_rows_ref[...], receivers)
    taps_low[...] = lay_taps(tap_low_ref[...], slot_rows_ref[...], receivers)
    signal[:, 0:LANES] = jnp.zeros((rows, LANES), jnp.bfloat16)
    signal[:, width : width + LANES] = jnp.zeros((rows, LANES), jnp.bfloat16)
    piece = 512

    def direct(step, _):
        start = pl.multiple_of(step * piece, LANES)
        window = shifted[:, pl.ds(start, LANES + piece)]
        spread = jnp.dot(taps_high[...], window, preferred_element_type=jnp.float32) + jnp.dot(
            taps_low[...], window, preferred_element_type=jnp.float32
        )
        echo = echo_ref[:, pl.ds(start, piece)].astype(jnp.float32)
        heard = (echo + coarse_sum(spread)).astype(jnp.bfloat16)
        received_ref[:, pl.ds(start, piece)] = heard
        after = pl.multiple_of(start + LANES, LANES)
        signal[0 : 2 * receivers, pl.ds(after, piece)] = heard
        signal[2 * receivers : rows, pl.ds(after, piece)] = refs_ref[:, pl.ds(after, piece)]
        return 0

    lax.fori_loop(0, length // piece, direct, 0)
    outer[...] = jnp.zeros(outer.shape, jnp.float32)
    span = 640

    def correlate(step, _):
        start = pl.multiple_of(step * span, LANES)
        ahead = signal[:, pl.ds(start, span + LANES)].astype(jnp.float32)
        moved = [ahead[:, :span].astype(jnp.bfloat16)]
        for coarse in range(1, COARSE):
            moved.append(
                pltpu.roll(ahead, span + LANES - coarse * FINE, 1)[:, :span].astype(jnp.bfloat16)
            )
        outer[...] += lax.dot_general(
            jnp.concatenate(moved, axis=0),
            shifted[:, pl.ds(start, span)],
            (((1,), (1,)), ((), ())),
            preferred_element_type=jnp.float32,
        )
        return 0

    lax.fori_loop(0, width // span, correlate, 0)
    scale = 1.0 / 262144.0
    lane = iota((1, LANES), 1)
    half = receivers
    for slot in range(16):
        base = (slot // 8) * 16 + slot % 8
        total = jnp.zeros((receivers + 16, LANES), jnp.float32)
        for coarse in range(COARSE):
            top = coarse * rows

            def part(out_part, in_part):
                col = (base + in_part * 8) * FINE
                tile = slice(col // LANES * LANES, col // LANES * LANES + LANES)
                first = outer[top + out_part * half : top + (out_part + 1) * half, tile]
                low = top + 2 * half
                own = outer[low + 8 * out_part : low + 8 * out_part + 8, tile]
                other = outer[low + 16 + 8 * out_part : low + 24 + 8 * out_part, tile]
                return jnp.concatenate([first, own, other], axis=0)

            offset = (base * FINE) % LANES
            real = part(0, 0) + part(1, 1)
            imag = part(1, 0) - part(0, 1)
            real = pltpu.roll(real, (coarse * FINE - offset) % LANES, 1)
            imag = pltpu.roll(imag, (DELAYS + coarse * FINE - offset) % LANES, 1)
            total = jnp.where(lane >> 4 == coarse, real, total)
            total = jnp.where(lane >> 4 == COARSE + coarse, imag, total)
        total = total * scale
        tidy[slot * receivers : (slot + 1) * receivers, :] = total[:receivers]
        corr_ref[slot * 16 : (slot + 1) * 16, :] = total[receivers:]
    for k in range(PER_RECV):

        def pick(row, _):
            chosen = slot_ref[row, k] * receivers + row
            picked[pl.ds(row, 1), :] = tidy[pl.ds(chosen, 1), :]
            return 0

        lax.fori_loop(0, receivers, pick, 0, unroll=8)
        cross_ref[:, k * LANES : (k + 1) * LANES] = picked[...]


def receive(slot, tap_high, tap_low, slot_rows, refs, echoes):
    rows, length = echoes.shape
    receivers = rows // 2
    width = length + LANES
    smem = pl.BlockSpec(memory_space=pltpu.SMEM)
    vmem = pl.BlockSpec(memory_space=pltpu.VMEM)
    all_rows = rows + 32
    return pl.pallas_call(
        receive_kernel,
        out_shape=(
            jax.ShapeDtypeStruct((rows, length), jnp.bfloat16),
            jax.ShapeDtypeStruct((receivers, PER_RECV * LANES), jnp.float32),
            jax.ShapeDtypeStruct((256, LANES), jnp.float32),
        ),
        in_specs=[smem, vmem, vmem, vmem, vmem, vmem],
        out_specs=(vmem, vmem, vmem),
        scratch_shapes=[
            pltpu.VMEM((32 * FINE, width), jnp.bfloat16),
            pltpu.VMEM((COARSE * rows, 32 * FINE), jnp.bfloat16),
            pltpu.VMEM((COARSE * rows, 32 * FINE), jnp.bfloat16),
            pltpu.VMEM((all_rows, width + LANES), jnp.bfloat16),
            pltpu.VMEM((COARSE * all_rows, 32 * FINE), jnp.float32),
            pltpu.VMEM((16 * receivers, LANES), jnp.float32),
            pltpu.VMEM((receivers, LANES), jnp.float32),
        ],
        compiler_params=pltpu.CompilerParams(vmem_limit_bytes=48 * 2**20),
        name="receive",
    )(slot, tap_high, tap_low, slot_rows, refs, echoes)


def cancel_kernel(tap_ref, slot_rows_ref, refs_ref, received_ref, out_ref, shifted, taps):
    receivers = received_ref.shape[0] // 2
    length = received_ref.shape[1]
    build_shifted(refs_ref, shifted)
    taps[...] = lay_taps(tap_ref[...], slot_rows_ref[...], receivers)
    piece = 512

    def project(step, _):
        start = pl.multiple_of(step * piece, LANES)
        spread = jnp.dot(
            taps[...], shifted[:, pl.ds(start, LANES + piece)], preferred_element_type=jnp.float32
        )
        received = received_ref[:, pl.ds(start, piece)].astype(jnp.float32)
        out_ref[:, pl.ds(start, piece)] = (received - coarse_sum(spread)).astype(jnp.bfloat16)
        return 0

    lax.fori_loop(0, length // piece, project, 0)


def cancel(taps, slot_rows, refs, received):
    rows, length = received.shape
    vmem = pl.BlockSpec(memory_space=pltpu.VMEM)
    return pl.pallas_call(
        cancel_kernel,
        out_shape=jax.ShapeDtypeStruct((rows, length), jnp.bfloat16),
        in_specs=[vmem] * 4,
        out_specs=vmem,
        scratch_shapes=[
            pltpu.VMEM((32 * FINE, length + LANES), jnp.bfloat16),
            pltpu.VMEM((COARSE * rows, 32 * FINE), jnp.bfloat16),
        ],
        compiler_params=pltpu.CompilerParams(vmem_limit_bytes=40 * 2**20),
        name="cancel",
    )(taps, slot_rows, refs, received)


def times_i(packed):
    sign = jnp.where(iota((1, LANES), 1) < DELAYS, -1.0, 1.0)
    count = packed.shape[1] // LANES
    blocks = [
        pltpu.roll(packed[:, b * LANES : (b + 1) * LANES], DELAYS, 1) * sign for b in range(count)
    ]
    return blocks[0] if count == 1 else jnp.concatenate(blocks, axis=1)


def inverse(block):
    size = block.shape[0]
    lane = iota((1, LANES), 1)
    sub = iota((size, 1), 0)
    sign = jnp.where(lane < DELAYS, -1.0, 1.0)

    def spread(column):
        return jnp.broadcast_to(column, (size, LANES))

    col_re = spread(block[:, 0:1])
    col_im = spread(block[:, DELAYS : DELAYS + 1])
    for p in range(size):
        last = p + 1 == size
        if not last:
            next_re = spread(block[:, p + 1 : p + 2])
            next_im = spread(block[:, DELAYS + p + 1 : DELAYS + p + 2])
        row = block[p : p + 1, :]
        over = 1.0 / col_re[p : p + 1, :]
        row = jnp.where(lane == p, 1.0, jnp.where(lane == DELAYS + p, 0.0, row))
        turned = pltpu.roll(row, DELAYS, 1) * sign
        row = row * over
        turned = turned * over
        if not last:
            fac_re = col_re[p + 1 : p + 2, :] * over
            fac_im = -col_im[p + 1 : p + 2, :] * over
            next_re = next_re - col_re * fac_re + col_im * fac_im
            next_im = next_im - col_re * fac_im - col_im * fac_re
            next_re = jnp.where(sub == p, fac_re, next_re)
            next_im = jnp.where(sub == p, fac_im, next_im)
        block = jnp.where((lane & (DELAYS - 1)) == p, 0.0, block)
        block = block - col_re * row - col_im * turned
        block = jnp.where(sub == p, row, block)
        if not last:
            col_re, col_im = next_re, next_im
    return block


def exact_dot(left, right):
    return jnp.dot(left, right, precision=HIGHEST, preferred_element_type=jnp.float32)


def solve_kernel(slot_ref, corr_ref, cross_ref, out_ref, system, pairs):
    count = PER_RECV
    size = DELAYS
    for k in range(count):
        for l in range(count):
            row = k * count + l
            ahead = slot_ref[k] * 16 + slot_ref[l]
            behind = slot_ref[l] * 16 + slot_ref[k]
            pairs[row : row + 1, 0:LANES] = corr_ref[pl.ds(ahead, 1), :]
            pairs[row : row + 1, LANES : 2 * LANES] = corr_ref[pl.ds(behind, 1), :]
    pairs[count * count :, :] = jnp.zeros((pairs.shape[0] - count * count, 2 * LANES), jnp.float32)
    src = iota((2 * LANES, 2 * LANES), 0)
    dst = iota((2 * LANES, 2 * LANES), 1)
    x = dst & (LANES - 1)
    imag = dst >> 7
    from_ahead = jnp.where(x > size, imag * size + LANES - x, jnp.where(x == 0, imag * size, -1))
    from_behind_lag = jnp.where((x > 0) & (x < size), LANES + imag * size + x, -1)
    order = jnp.where(src == from_ahead, 1.0, 0.0) + jnp.where(
        src == from_behind_lag, jnp.where(imag == 1, -1.0, 1.0), 0.0
    )
    circular = exact_dot(pairs[...], order)
    lane = iota((1, LANES), 1)
    sub = iota((size, 1), 0)
    for k in range(count):
        for l in range(count):
            row = k * count + l
            real = jnp.broadcast_to(circular[row : row + 1, 0:LANES], (size, LANES))
            imag_part = jnp.broadcast_to(circular[row : row + 1, LANES:], (size, LANES))
            real = pltpu.roll(real, 0, 1, stride=1, stride_axis=0)
            imag_part = pltpu.roll(imag_part, size, 1, stride=1, stride_axis=0)
            block = jnp.where(lane < size, real, imag_part)
            if k == l:
                block = block + jnp.where(lane == sub, loading, 0.0)
            system[k * size : (k + 1) * size, l * LANES : (l + 1) * LANES] = block
    lane_sq = iota((LANES, LANES), 1)
    sub_sq = iota((LANES, LANES), 0)
    gather = jnp.where(lane_sq == (sub_sq >> 6) * size, 1.0, 0.0)
    on_diag = (lane & (size - 1)) == sub
    for k in range(count):
        spread = jnp.where(on_diag, cross_ref[:, k * LANES : (k + 1) * LANES], 0.0)
        system[k * size : (k + 1) * size, count * LANES :] = exact_dot(spread, gather)
    for i in range(count):
        mine = slice(i * size, (i + 1) * size)
        col = slice(i * LANES, (i + 1) * LANES)
        rest = slice((i + 1) * LANES, (count + 1) * LANES)
        over = inverse(system[mine, col])
        right = system[mine, rest]
        scaled = exact_dot(over, jnp.concatenate([right, times_i(right)], axis=0))
        both = jnp.concatenate([scaled, times_i(scaled)], axis=0)
        system[:, rest] = system[:, rest] - exact_dot(system[:, col], both)
        system[mine, rest] = scaled
    scatter = jnp.where(sub_sq == (lane_sq >> 6) * size, 1.0, 0.0)
    ones = jnp.ones((8, size), jnp.float32)
    for k in range(count):
        found = exact_dot(system[k * size : (k + 1) * size, count * LANES :], scatter)
        row = exact_dot(ones, jnp.where(on_diag, found, 0.0))
        out_ref[:, k * LANES : (k + 1) * LANES] = row[0:1]


def solve(slot, corr, cross):
    smem = pl.BlockSpec(memory_space=pltpu.SMEM)
    vmem = pl.BlockSpec(memory_space=pltpu.VMEM)
    size = PER_RECV * DELAYS
    return pl.pallas_call(
        solve_kernel,
        out_shape=jax.ShapeDtypeStruct((1, PER_RECV * LANES), jnp.float32),
        in_specs=[smem, vmem, vmem],
        out_specs=vmem,
        scratch_shapes=[
            pltpu.VMEM((size, (PER_RECV + 1) * LANES), jnp.float32),
            pltpu.VMEM((40, 2 * LANES), jnp.float32),
        ],
        name="solve",
    )(slot, corr, cross)


def local(symbols, incidence, delays, gains, echoes):
    owned, length = symbols.shape
    chan_count = lax.axis_size("chan")
    chan_index = lax.axis_index("chan")
    tm_count = lax.axis_size("tm")
    tm_index = lax.axis_index("tm")
    recv_count = echoes.shape[1]
    own = remodulate(symbols).reshape(2 * owned, length)
    following = passed_along(own, "chan", -1)
    window = jnp.concatenate([own, following], axis=0)
    previous = from_behind(window[:, length - LANES :], "tm", 1)
    refs = jnp.concatenate([previous, window], axis=1)
    owner_chan = incidence // owned
    slot = (owner_chan - chan_index) % chan_count * owned + incidence % owned
    slot_rows = jnp.broadcast_to(
        slot.T.reshape(PER_RECV * recv_count, 1), (PER_RECV * recv_count, LANES)
    )
    lag = jnp.arange(LANES, dtype=jnp.int32)
    gain_rows = jnp.where(
        lag < DELAYS,
        gains[0].T.reshape(PER_RECV * recv_count, 1),
        gains[1].T.reshape(PER_RECV * recv_count, 1),
    )
    gain_taps = jnp.where(
        delays.T.reshape(PER_RECV * recv_count, 1) == (lag & (DELAYS - 1)), gain_rows, 0.0
    )
    tap_high = lax.reduce_precision(gain_taps, 8, 7)
    tap_low = (gain_taps - tap_high).astype(jnp.bfloat16)
    received, cross, corr = receive(
        slot, tap_high.astype(jnp.bfloat16), tap_low, slot_rows, refs, echoes.reshape(2 * recv_count, length)
    )
    share = recv_count // tm_count
    corr_share = corr.size // tm_count
    parts = jnp.concatenate([cross, corr.reshape(tm_count, corr_share)], axis=1)
    parts = jnp.sum(lax.all_to_all(parts, "tm", 0, 0, tiled=True), axis=0, keepdims=True)
    my_cross = parts[:, : PER_RECV * LANES]
    my_corr = jnp.broadcast_to(parts[:, PER_RECV * LANES :], (tm_count, corr_share))
    corr = lax.all_to_all(my_corr, "tm", 0, 0, tiled=True).reshape(256, LANES)
    my_slot = lax.dynamic_slice_in_dim(slot, tm_index * share, share, 0).reshape(PER_RECV)
    mine = solve(my_slot, corr, my_cross)
    solved = lax.all_to_all(
        jnp.broadcast_to(mine, (tm_count, PER_RECV * LANES)), "tm", 0, 0, tiled=True
    ).reshape(recv_count, PER_RECV, 2, DELAYS)
    weights = jnp.transpose(solved, (2, 0, 1, 3)).reshape(2, recv_count, PER_RECV * DELAYS)
    taps = jnp.transpose(solved.astype(jnp.bfloat16), (1, 0, 2, 3)).reshape(
        PER_RECV * recv_count, LANES
    )
    cancelled = cancel(taps, slot_rows, refs, received).reshape(2, recv_count, length)
    return (cancelled, weights)


def solution(mesh):
    in_specs = (
        P("chan", "tm"),
        P("chan", None),
        P("chan", None),
        P(None, "chan", None),
        P(None, "chan", "tm"),
    )
    out_specs = (P(None, "chan", "tm"), P(None, "chan", None))
    return jax.shard_map(local, mesh=mesh, in_specs=in_specs, out_specs=out_specs, check_vma=False)
```

```python
import math

import jax
import jax.numpy as jnp
from jax import lax
from jax.experimental import pallas as pl
from jax.experimental.pallas import tpu as pltpu
from jax.sharding import PartitionSpec as P

ACTIVE = 6817
DELAYS = 64
PER_RECV = 6
LANES = 128
FINE = 16
COARSE = DELAYS // FINE
PANEL = 4
SPAN = 640
PIECE = 1024
RECEIVE_VMEM = 56 * 2**20


loading = 0.1
HIGHEST = lax.Precision.HIGHEST


def passed_along(array, axis, by):
    peers = lax.axis_size(axis)
    return lax.ppermute(array, axis, [(i, (i + by) % peers) for i in range(peers)])


def from_behind(block, axis, distance):
    devices = range(lax.axis_size(axis))
    route = [(i - distance, i) for i in devices if i - distance in devices]
    return lax.ppermute(block, axis, route)


def rotation_angle_grid(row_count, col_count, period):
    product = (
        jnp.arange(row_count, dtype=jnp.int32)[:, None]
        * jnp.arange(col_count, dtype=jnp.int32)[None, :]
    )
    phases = (product % period).astype(jnp.float32) * (2.0 * math.pi / period)
    return (jnp.cos(phases), jnp.sin(phases))


def complex_multiply_result(pattern, left_pair, right_pair):
    real_part = jnp.einsum(pattern, left_pair[0], right_pair[0], precision=HIGHEST) - jnp.einsum(
        pattern, left_pair[1], right_pair[1], precision=HIGHEST
    )
    imag_part = jnp.einsum(pattern, left_pair[0], right_pair[1], precision=HIGHEST) + jnp.einsum(
        pattern, left_pair[1], right_pair[0], precision=HIGHEST
    )
    return (real_part, imag_part)


def remodulate(symbols):
    emitter_number, length = symbols.shape
    column_entries = 128
    increment_spacing = length // column_entries
    inphase_amplitude = (2 * (symbols % 8) - 7).astype(jnp.float32) / math.sqrt(42.0)
    quadrature_amplitude = (2 * (symbols // 8) - 7).astype(jnp.float32) / math.sqrt(42.0)
    subcarrier = jnp.arange(length, dtype=jnp.int32) - length // 2
    occupied_tones = (jnp.abs(subcarrier) <= (ACTIVE - 1) // 2).astype(jnp.float32)
    tone_symbols = (
        (inphase_amplitude * occupied_tones).reshape(
            emitter_number, increment_spacing, column_entries
        ),
        (quadrature_amplitude * occupied_tones).reshape(
            emitter_number, increment_spacing, column_entries
        ),
    )
    partial_result = complex_multiply_result(
        "mb,nbd->nmd",
        rotation_angle_grid(increment_spacing, increment_spacing, increment_spacing),
        tone_symbols,
    )
    twiddle = rotation_angle_grid(increment_spacing, column_entries, length)
    partial_result = (
        partial_result[0] * twiddle[0] - partial_result[1] * twiddle[1],
        partial_result[0] * twiddle[1] + partial_result[1] * twiddle[0],
    )
    frequency_spectrum = complex_multiply_result(
        "pho,oj->phj",
        partial_result,
        rotation_angle_grid(column_entries, column_entries, column_entries),
    )
    alternate = (1 - 2 * (jnp.arange(length, dtype=jnp.int32) % 2)).astype(jnp.float32) / math.sqrt(
        ACTIVE
    )
    real_part = (
        jnp.swapaxes(frequency_spectrum[0], 1, 2).reshape(emitter_number, length) * alternate
    )
    imag_part = (
        jnp.swapaxes(frequency_spectrum[1], 1, 2).reshape(emitter_number, length) * alternate
    )
    return jnp.stack([real_part, imag_part], axis=0).astype(jnp.bfloat16)


def iota(shape, axis):
    return lax.broadcasted_iota(jnp.int32, shape, axis)


def copy_of(source, target, sems, step, start, size):
    cols = pl.ds(pl.multiple_of(start, LANES), size)
    return pltpu.make_async_copy(source.at[:, cols], target.at[:, cols], sems.at[step])


def build_shifted(ref_ref, shifted_ref, kept_ref, sems):
    rows, width = ref_ref.shape
    piece = SPAN

    def one_piece(step, _):
        start = pl.multiple_of(step * piece, LANES)
        before = pl.multiple_of(jnp.maximum(start - LANES, 0), LANES)
        first = ref_ref[:, pl.ds(before, LANES)].astype(jnp.float32)
        body = ref_ref[:, pl.ds(start, piece)].astype(jnp.float32)
        source = jnp.concatenate([first, body], axis=1)
        for row in range(rows):
            spread = jnp.broadcast_to(source[row : row + 1, :], (FINE, LANES + piece))
            rolled = pltpu.roll(spread, 0, 1, stride=1, stride_axis=0)
            shifted_ref[row * FINE : (row + 1) * FINE, pl.ds(start, piece)] = rolled[
                :, LANES:
            ].astype(jnp.bfloat16)
        copy_of(shifted_ref, kept_ref, sems, step, start, piece).start()
        return 0

    lax.fori_loop(0, width // piece, one_piece, 0)


def lay_taps(tap_rows, slot_rows, receivers):
    cols = 32 * FINE
    lane = iota((LANES, cols), 1)
    source = iota((LANES, cols), 0)
    fine = lane & (FINE - 1)
    in_part = (lane >> 7) & 1
    col_slot = ((iota((1, cols), 1) >> 8) << 3) + ((iota((1, cols), 1) >> 4) & 7)
    blocks = []
    for coarse in range(COARSE):
        for out_part in range(2):
            part = in_part ^ out_part
            sign = jnp.where((in_part == 1) & (out_part == 0), -1.0, 1.0)
            spread = jnp.where(source == part * DELAYS + coarse * FINE + fine, sign, 0.0)
            wide = jnp.dot(
                tap_rows, spread.astype(jnp.bfloat16), preferred_element_type=jnp.float32
            )
            total = jnp.zeros((receivers, cols), jnp.float32)
            for k in range(PER_RECV):
                rows = slice(k * receivers, (k + 1) * receivers)
                total = total + jnp.where(
                    slot_rows[rows, 0:1] == col_slot, wide[rows, :], 0.0
                )
            blocks.append(total)
    return jnp.concatenate(blocks, axis=0).astype(jnp.bfloat16)


def coarse_sum(spread):
    rows = spread.shape[0] // COARSE
    total = spread[:rows, LANES:]
    for coarse in range(1, COARSE):
        total = total + pltpu.roll(spread[coarse * rows : (coarse + 1) * rows], coarse * FINE, 1)[:, LANES:]
    return total


def moved_ahead(ahead, span):
    moved = [ahead[:, :span].astype(jnp.bfloat16)]
    for coarse in range(1, COARSE):
        moved.append(
            pltpu.roll(ahead, span + LANES - coarse * FINE, 1)[:, :span].astype(jnp.bfloat16)
        )
    return jnp.concatenate(moved, axis=0)


def by_lag(read, rows, store):
    lane = iota((1, LANES), 1)
    for block in range(2):

        def one_slot(j, _, block=block):
            total = jnp.zeros((rows, LANES), jnp.float32)
            for coarse in range(COARSE):
                real = read(coarse, 0, 2 * block) + read(coarse, 1, 2 * block + 1)
                imag = read(coarse, 1, 2 * block) - read(coarse, 0, 2 * block + 1)
                place = coarse * FINE + LANES - j * FINE
                real = pltpu.roll(real, place, 1)
                imag = pltpu.roll(imag, place + DELAYS, 1)
                total = jnp.where(lane >> 4 == coarse, real, total)
                total = jnp.where(lane >> 4 == COARSE + coarse, imag, total)
            store(block * 8 + j, total * (1.0 / 262144.0))
            return 0

        lax.fori_loop(0, 8, one_slot, 0)


def fetch_all(kept_ref, shifted, sems, step_size):
    width = kept_ref.shape[1]
    lead = width % step_size
    steps = width // step_size
    if lead:
        copy_of(kept_ref, shifted, sems, steps, 0, lead).start()
    for step in range(steps):
        copy_of(kept_ref, shifted, sems, step, lead + step * step_size, step_size).start()
    if lead:
        copy_of(kept_ref, shifted, sems, steps, 0, lead).wait()

    def arrive(step):
        copy_of(kept_ref, shifted, sems, step, lead + step * step_size, step_size).wait()

    return arrive


def receive_kernel(
    slot_ref, tap_high_ref, tap_low_ref, slot_rows_ref, refs_ref, echo_ref,
    received_ref, cross_ref, corr_ref, kept_ref,
    shifted, taps_high, taps_low, signal, outer, flipped, tidy, picked, sems,
):
    receivers = echo_ref.shape[0] // 2
    length = echo_ref.shape[1]
    width = length + LANES
    heard_rows = 2 * receivers
    rows = heard_rows + 32
    build_shifted(refs_ref, shifted, kept_ref, sems)
    taps_high[...] = lay_taps(tap_high_ref[...], slot_rows_ref[...], receivers)
    taps_low[...] = lay_taps(tap_low_ref[...], slot_rows_ref[...], receivers)
    signal[:, 0:LANES] = jnp.zeros((rows, LANES), jnp.bfloat16)
    signal[heard_rows:rows, LANES:width] = refs_ref[:, LANES:width]
    signal[:, width : width + LANES] = jnp.zeros((rows, LANES), jnp.bfloat16)

    def direct(step, _):
        start = pl.multiple_of(step * PIECE, LANES)
        window = shifted[:, pl.ds(start, LANES + PIECE)]
        spread = jnp.dot(taps_high[...], window, preferred_element_type=jnp.float32) + jnp.dot(
            taps_low[...], window, preferred_element_type=jnp.float32
        )
        echo = echo_ref[:, pl.ds(start, PIECE)].astype(jnp.float32)
        heard = (echo + coarse_sum(spread)).astype(jnp.bfloat16)
        received_ref[:, pl.ds(start, PIECE)] = heard
        signal[0:heard_rows, pl.ds(pl.multiple_of(start + LANES, LANES), PIECE)] = heard
        return 0

    lax.fori_loop(0, length // PIECE, direct, 0)
    outer[...] = jnp.zeros(outer.shape, jnp.float32)

    def correlate(step, _):
        start = pl.multiple_of(step * SPAN, LANES)
        outer[...] += lax.dot_general(
            shifted[:, pl.ds(start, SPAN)],
            moved_ahead(signal[:, pl.ds(start, SPAN + LANES)].astype(jnp.float32), SPAN),
            (((1,), (1,)), ((), ())),
            preferred_element_type=jnp.float32,
        )
        return 0

    lax.fori_loop(0, width // SPAN, correlate, 0)
    flipped[...] = jnp.transpose(outer[...])

    def read(coarse, out_part, tile):
        cols = slice(tile * LANES, (tile + 1) * LANES)
        top = coarse * rows + receivers * out_part
        low = coarse * rows + heard_rows + 8 * out_part
        return jnp.concatenate(
            [
                flipped[top : top + receivers, cols],
                flipped[low : low + 8, cols],
                flipped[low + 16 : low + 24, cols],
            ],
            axis=0,
        )

    def store(slot, lags):
        tidy[pl.ds(pl.multiple_of(slot * receivers, receivers), receivers), :] = lags[:receivers]
        corr_ref[pl.ds(pl.multiple_of(slot * 16, 16), 16), :] = lags[receivers:]

    by_lag(read, receivers + 16, store)

    def pick(row, _):
        for k in range(PER_RECV):
            chosen = slot_ref[row, k] * receivers + row
            picked[pl.ds(k * receivers + row, 1), :] = tidy[pl.ds(chosen, 1), :]
        return 0

    lax.fori_loop(0, receivers, pick, 0, unroll=4)
    low = iota((1, LANES), 1) < DELAYS
    for pair in range(PER_RECV // 2):
        even = picked[2 * pair * receivers : (2 * pair + 1) * receivers, :]
        odd = picked[(2 * pair + 1) * receivers : (2 * pair + 2) * receivers, :]
        cross_ref[:, pair * LANES : (pair + 1) * LANES] = jnp.where(
            low, even, pltpu.roll(odd, DELAYS, 1)
        )
        pair += PER_RECV // 2
        cross_ref[:, pair * LANES : (pair + 1) * LANES] = jnp.where(
            low, pltpu.roll(even, DELAYS, 1), odd
        )

    def sent(step, _):
        copy_of(shifted, kept_ref, sems, step, step * SPAN, SPAN).wait()
        return 0

    lax.fori_loop(0, width // SPAN, sent, 0)


def receive(slot, tap_high, tap_low, slot_rows, refs, echoes):
    rows, length = echoes.shape
    receivers = rows // 2
    width = length + LANES
    smem = pl.BlockSpec(memory_space=pltpu.SMEM)
    vmem = pl.BlockSpec(memory_space=pltpu.VMEM)
    products = COARSE * (rows + 32)
    return pl.pallas_call(
        receive_kernel,
        out_shape=(
            jax.ShapeDtypeStruct((rows, length), jnp.bfloat16),
            jax.ShapeDtypeStruct((receivers, PER_RECV * LANES), jnp.float32),
            jax.ShapeDtypeStruct((256, LANES), jnp.float32),
            jax.ShapeDtypeStruct((32 * FINE, width), jnp.bfloat16),
        ),
        in_specs=[smem, vmem, vmem, vmem, vmem, vmem],
        out_specs=(vmem, vmem, vmem, pl.BlockSpec(memory_space=pl.ANY)),
        scratch_shapes=[
            pltpu.VMEM((32 * FINE, width), jnp.bfloat16),
            pltpu.VMEM((COARSE * rows, 32 * FINE), jnp.bfloat16),
            pltpu.VMEM((COARSE * rows, 32 * FINE), jnp.bfloat16),
            pltpu.VMEM((rows + 32, width + LANES), jnp.bfloat16),
            pltpu.VMEM((32 * FINE, products), jnp.float32),
            pltpu.VMEM((products, 32 * FINE), jnp.float32),
            pltpu.VMEM((16 * receivers, LANES), jnp.float32),
            pltpu.VMEM((PER_RECV * receivers, LANES), jnp.float32),
            pltpu.SemaphoreType.DMA((width // SPAN,)),
        ],
        compiler_params=pltpu.CompilerParams(vmem_limit_bytes=RECEIVE_VMEM),
        name="receive",
    )(slot, tap_high, tap_low, slot_rows, refs, echoes)


def cancel_kernel(
    tap_ref, slot_rows_ref, kept_ref, received_ref, out_ref, taps, shifted, sems
):
    receivers = received_ref.shape[0] // 2
    length = received_ref.shape[1]
    arrive = fetch_all(kept_ref, shifted, sems, PIECE)
    taps[...] = lay_taps(tap_ref[...], slot_rows_ref[...], receivers)
    piece = PIECE

    def project(step, _):
        start = pl.multiple_of(step * piece, LANES)
        arrive(step)
        spread = jnp.dot(
            taps[...], shifted[:, pl.ds(start, LANES + piece)], preferred_element_type=jnp.float32
        )
        received = received_ref[:, pl.ds(start, piece)].astype(jnp.float32)
        out_ref[:, pl.ds(start, piece)] = (received - coarse_sum(spread)).astype(jnp.bfloat16)
        return 0

    lax.fori_loop(0, length // piece, project, 0)


def cancel(taps, slot_rows, shifted, received):
    rows, length = received.shape
    vmem = pl.BlockSpec(memory_space=pltpu.VMEM)
    return pl.pallas_call(
        cancel_kernel,
        out_shape=jax.ShapeDtypeStruct((rows, length), jnp.bfloat16),
        in_specs=[vmem, vmem, pl.BlockSpec(memory_space=pl.ANY), vmem],
        out_specs=vmem,
        scratch_shapes=[
            pltpu.VMEM((COARSE * rows, 32 * FINE), jnp.bfloat16),
            pltpu.VMEM((32 * FINE, length + LANES), jnp.bfloat16),
            pltpu.SemaphoreType.DMA((length // PIECE + 1,)),
        ],
        compiler_params=pltpu.CompilerParams(vmem_limit_bytes=RECEIVE_VMEM),
        name="cancel",
    )(taps, slot_rows, shifted, received)


def times_i(packed):
    sign = jnp.where(iota((1, LANES), 1) < DELAYS, -1.0, 1.0)
    count = packed.shape[1] // LANES
    blocks = [
        pltpu.roll(packed[:, b * LANES : (b + 1) * LANES], DELAYS, 1) * sign for b in range(count)
    ]
    return blocks[0] if count == 1 else jnp.concatenate(blocks, axis=1)


def inverse(block):
    size = block.shape[0]
    lane = iota((1, LANES), 1)
    low = lane & (DELAYS - 1)
    sub = iota((size, 1), 0)
    sign = jnp.where(lane < DELAYS, -1.0, 1.0)

    def spread(column):
        return jnp.broadcast_to(block[:, column : column + 1], (size, LANES))

    for first in range(0, size, PANEL):
        col_re = [spread(first + t) for t in range(PANEL)]
        col_im = [spread(DELAYS + first + t) for t in range(PANEL)]
        rows = [block[first + t : first + t + 1, :] for t in range(PANEL)]
        turned_rows = [pltpu.roll(row, DELAYS, 1) * sign for row in rows]
        block = jnp.where((low >= first) & (low < first + PANEL), 0.0, block)
        for t in range(PANEL):
            p = first + t
            over = 1.0 / col_re[t][p : p + 1, :]
            row = jnp.where(lane == p, 1.0, jnp.where(lane == DELAYS + p, 0.0, rows[t])) * over
            turned = (
                jnp.where(lane == DELAYS + p, 1.0, jnp.where(lane == p, 0.0, turned_rows[t])) * over
            )
            for u in range(t + 1, PANEL):
                q = first + u
                below_re = col_re[t][q : q + 1, :]
                below_im = col_im[t][q : q + 1, :]
                fac_re = below_re * over
                fac_im = -below_im * over
                next_re = col_re[u] - col_re[t] * fac_re + col_im[t] * fac_im
                next_im = col_im[u] - col_re[t] * fac_im - col_im[t] * fac_re
                col_re[u] = jnp.where(sub == p, fac_re, next_re)
                col_im[u] = jnp.where(sub == p, fac_im, next_im)
                rows[u] = jnp.where(low == p, 0.0, rows[u]) - below_re * row - below_im * turned
                turned_rows[u] = (
                    jnp.where(low == p, 0.0, turned_rows[u]) - below_re * turned + below_im * row
                )
            later = (low > p) & (low < first + PANEL)
            row = jnp.where(later, 0.0, row)
            turned = jnp.where(later, 0.0, turned)
            block = block - col_re[t] * row - col_im[t] * turned
            block = jnp.where(sub == p, row, block)
    return block


def exact_dot(left, right):
    return jnp.dot(left, right, precision=HIGHEST, preferred_element_type=jnp.float32)


def solve_kernel(slot_ref, corr_ref, cross_ref, out_ref, system, pairs):
    count = PER_RECV
    size = DELAYS
    for k in range(count):
        for l in range(count):
            row = k * count + l
            ahead = slot_ref[k] * 16 + slot_ref[l]
            behind = slot_ref[l] * 16 + slot_ref[k]
            pairs[row : row + 1, 0:LANES] = corr_ref[pl.ds(ahead, 1), :]
            pairs[row : row + 1, LANES : 2 * LANES] = corr_ref[pl.ds(behind, 1), :]
    pairs[count * count :, :] = jnp.zeros((pairs.shape[0] - count * count, 2 * LANES), jnp.float32)
    src = iota((2 * LANES, 2 * LANES), 0)
    dst = iota((2 * LANES, 2 * LANES), 1)
    x = dst & (LANES - 1)
    imag = dst >> 7
    from_ahead = jnp.where(x > size, imag * size + LANES - x, jnp.where(x == 0, imag * size, -1))
    from_behind_lag = jnp.where((x > 0) & (x < size), LANES + imag * size + x, -1)
    order = jnp.where(src == from_ahead, 1.0, 0.0) + jnp.where(
        src == from_behind_lag, jnp.where(imag == 1, -1.0, 1.0), 0.0
    )
    circular = exact_dot(pairs[...], order)
    lane = iota((1, LANES), 1)
    sub = iota((size, 1), 0)
    for k in range(count):
        for l in range(count):
            row = k * count + l
            real = jnp.broadcast_to(circular[row : row + 1, 0:LANES], (size, LANES))
            imag_part = jnp.broadcast_to(circular[row : row + 1, LANES:], (size, LANES))
            real = pltpu.roll(real, 0, 1, stride=1, stride_axis=0)
            imag_part = pltpu.roll(imag_part, size, 1, stride=1, stride_axis=0)
            block = jnp.where(lane < size, real, imag_part)
            if k == l:
                block = block + jnp.where(lane == sub, loading, 0.0)
            system[k * size : (k + 1) * size, l * LANES : (l + 1) * LANES] = block
    unit = jnp.where(lane == sub, 1.0, 0.0)

    def eliminate(i, _):
        mine = pl.ds(pl.multiple_of(i * size, size), size)
        col = pl.ds(pl.multiple_of(i * LANES, LANES), LANES)
        over = inverse(system[mine, col])
        system[mine, col] = unit
        right = system[mine, :]
        scaled = exact_dot(over, jnp.concatenate([right, times_i(right)], axis=0))
        factors = system[:, col]
        system[:, col] = jnp.zeros((count * size, LANES), jnp.float32)
        both = jnp.concatenate([scaled, times_i(scaled)], axis=0)
        system[...] = system[...] - exact_dot(factors, both)
        system[mine, :] = scaled
        return 0

    lax.fori_loop(0, count, eliminate, 0)
    whole = count * size
    total = cross_ref[...]
    sides = jnp.concatenate(
        [total[:, :whole], total[:, whole:], jnp.zeros((6, whole), jnp.float32)], axis=0
    )
    found = exact_dot(sides, system[...])
    for k in range(count):
        by_real = found[0:1, k * LANES : (k + 1) * LANES]
        by_imag = found[1:2, k * LANES : (k + 1) * LANES]
        row = jnp.where(lane < size, by_real, -by_real) + pltpu.roll(by_imag, size, 1)
        out_ref[:, k * LANES : (k + 1) * LANES] = row


def solve(slot, corr, cross):
    smem = pl.BlockSpec(memory_space=pltpu.SMEM)
    vmem = pl.BlockSpec(memory_space=pltpu.VMEM)
    size = PER_RECV * DELAYS
    return pl.pallas_call(
        solve_kernel,
        out_shape=jax.ShapeDtypeStruct((1, PER_RECV * LANES), jnp.float32),
        in_specs=[smem, vmem, vmem],
        out_specs=vmem,
        scratch_shapes=[
            pltpu.VMEM((size, PER_RECV * LANES), jnp.float32),
            pltpu.VMEM((40, 2 * LANES), jnp.float32),
        ],
        compiler_params=pltpu.CompilerParams(vmem_limit_bytes=RECEIVE_VMEM),
        name="solve",
    )(slot, corr, cross)


def local(symbols, incidence, delays, gains, echoes):
    owned, length = symbols.shape
    chan_count = lax.axis_size("chan")
    chan_index = lax.axis_index("chan")
    tm_count = lax.axis_size("tm")
    tm_index = lax.axis_index("tm")
    recv_count = echoes.shape[1]
    own = remodulate(symbols).reshape(2 * owned, length)
    following = passed_along(own, "chan", -1)
    window = jnp.concatenate([own, following], axis=0)
    previous = from_behind(window[:, length - LANES :], "tm", 1)
    refs = jnp.concatenate([previous, window], axis=1)
    owner_chan = incidence // owned
    slot = (owner_chan - chan_index) % chan_count * owned + incidence % owned
    slot_rows = jnp.broadcast_to(
        slot.T.reshape(PER_RECV * recv_count, 1), (PER_RECV * recv_count, LANES)
    )
    lag = jnp.arange(LANES, dtype=jnp.int32)
    gain_rows = jnp.where(
        lag < DELAYS,
        gains[0].T.reshape(PER_RECV * recv_count, 1),
        gains[1].T.reshape(PER_RECV * recv_count, 1),
    )
    gain_taps = jnp.where(
        delays.T.reshape(PER_RECV * recv_count, 1) == (lag & (DELAYS - 1)), gain_rows, 0.0
    )
    tap_high = lax.reduce_precision(gain_taps, 8, 7)
    tap_low = (gain_taps - tap_high).astype(jnp.bfloat16)
    received, cross, corr, shifted = receive(
        slot,
        tap_high.astype(jnp.bfloat16),
        tap_low,
        slot_rows,
        refs,
        echoes.reshape(2 * recv_count, length),
    )
    share = recv_count // tm_count
    corr_share = corr.size // tm_count
    parts = jnp.concatenate([cross, corr.reshape(tm_count, corr_share)], axis=1)
    parts = jnp.sum(lax.all_to_all(parts, "tm", 0, 0, tiled=True), axis=0, keepdims=True)
    my_cross = parts[:, : PER_RECV * LANES]
    my_corr = jnp.broadcast_to(parts[:, PER_RECV * LANES :], (tm_count, corr_share))
    corr = lax.all_to_all(my_corr, "tm", 0, 0, tiled=True).reshape(256, LANES)
    my_slot = lax.dynamic_slice_in_dim(slot, tm_index * share, share, 0).reshape(PER_RECV)
    mine = jnp.broadcast_to(solve(my_slot, corr, my_cross), (tm_count, PER_RECV * LANES))
    solved = lax.all_to_all(mine, "tm", 0, 0, tiled=True).reshape(
        recv_count, PER_RECV, 2, DELAYS
    )
    weights = jnp.transpose(solved, (2, 0, 1, 3)).reshape(2, recv_count, PER_RECV * DELAYS)
    taps = jnp.transpose(solved.astype(jnp.bfloat16), (1, 0, 2, 3)).reshape(
        PER_RECV * recv_count, LANES
    )
    cancelled = cancel(taps, slot_rows, shifted, received).reshape(2, recv_count, length)
    return (cancelled, weights)


def solution(mesh):
    in_specs = (
        P("chan", "tm"),
        P("chan", None),
        P("chan", None),
        P(None, "chan", None),
        P(None, "chan", "tm"),
    )
    out_specs = (P(None, "chan", "tm"), P(None, "chan", None))
    return jax.shard_map(local, mesh=mesh, in_specs=in_specs, out_specs=out_specs, check_vma=False)
```

```python
import math

import jax
import jax.numpy as jnp
from jax import lax
from jax.experimental import pallas as pl
from jax.experimental.pallas import tpu as pltpu
from jax.sharding import PartitionSpec as P

ACTIVE = 6817
DELAYS = 64
PER_RECV = 6
LANES = 128
FINE = 16
COARSE = DELAYS // FINE
PARTS = PER_RECV * LANES + 1024
PANEL = 4
SPAN = 1664
PIECE = 2048
RECEIVE_VMEM = 56 * 2**20


loading = 0.1
HIGHEST = lax.Precision.HIGHEST


def passed_along(array, axis, by):
    peers = lax.axis_size(axis)
    return lax.ppermute(array, axis, [(i, (i + by) % peers) for i in range(peers)])


def from_behind(block, axis, distance):
    devices = range(lax.axis_size(axis))
    route = [(i - distance, i) for i in devices if i - distance in devices]
    return lax.ppermute(block, axis, route)


def rotation_angle_grid(row_count, col_count, period):
    product = (
        jnp.arange(row_count, dtype=jnp.int32)[:, None]
        * jnp.arange(col_count, dtype=jnp.int32)[None, :]
    )
    phases = (product % period).astype(jnp.float32) * (2.0 * math.pi / period)
    return (jnp.cos(phases), jnp.sin(phases))


def complex_multiply_result(pattern, left_pair, right_pair):
    real_part = jnp.einsum(pattern, left_pair[0], right_pair[0], precision=HIGHEST) - jnp.einsum(
        pattern, left_pair[1], right_pair[1], precision=HIGHEST
    )
    imag_part = jnp.einsum(pattern, left_pair[0], right_pair[1], precision=HIGHEST) + jnp.einsum(
        pattern, left_pair[1], right_pair[0], precision=HIGHEST
    )
    return (real_part, imag_part)


def remodulate(symbols):
    emitter_number, length = symbols.shape
    column_entries = 128
    increment_spacing = length // column_entries
    inphase_amplitude = (2 * (symbols % 8) - 7).astype(jnp.float32) / math.sqrt(42.0)
    quadrature_amplitude = (2 * (symbols // 8) - 7).astype(jnp.float32) / math.sqrt(42.0)
    subcarrier = jnp.arange(length, dtype=jnp.int32) - length // 2
    occupied_tones = (jnp.abs(subcarrier) <= (ACTIVE - 1) // 2).astype(jnp.float32)
    tone_symbols = (
        (inphase_amplitude * occupied_tones).reshape(
            emitter_number, increment_spacing, column_entries
        ),
        (quadrature_amplitude * occupied_tones).reshape(
            emitter_number, increment_spacing, column_entries
        ),
    )
    partial_result = complex_multiply_result(
        "mb,nbd->nmd",
        rotation_angle_grid(increment_spacing, increment_spacing, increment_spacing),
        tone_symbols,
    )
    twiddle = rotation_angle_grid(increment_spacing, column_entries, length)
    partial_result = (
        partial_result[0] * twiddle[0] - partial_result[1] * twiddle[1],
        partial_result[0] * twiddle[1] + partial_result[1] * twiddle[0],
    )
    frequency_spectrum = complex_multiply_result(
        "pho,oj->phj",
        partial_result,
        rotation_angle_grid(column_entries, column_entries, column_entries),
    )
    alternate = (1 - 2 * (jnp.arange(length, dtype=jnp.int32) % 2)).astype(jnp.float32) / math.sqrt(
        ACTIVE
    )
    real_part = (
        jnp.swapaxes(frequency_spectrum[0], 1, 2).reshape(emitter_number, length) * alternate
    )
    imag_part = (
        jnp.swapaxes(frequency_spectrum[1], 1, 2).reshape(emitter_number, length) * alternate
    )
    return jnp.stack([real_part, imag_part], axis=0).astype(jnp.bfloat16)


def iota(shape, axis):
    return lax.broadcasted_iota(jnp.int32, shape, axis)


def copy_of(source, target, sems, step, start, size):
    cols = pl.ds(pl.multiple_of(start, LANES), size)
    return pltpu.make_async_copy(source.at[:, cols], target.at[:, cols], sems.at[step])


def build_shifted(ref_ref, shifted_ref, kept_ref, sems):
    rows, width = ref_ref.shape
    piece = SPAN

    def one_piece(step, _):
        start = pl.multiple_of(step * piece, LANES)
        before = pl.multiple_of(jnp.maximum(start - LANES, 0), LANES)
        first = ref_ref[:, pl.ds(before, LANES)].astype(jnp.float32)
        body = ref_ref[:, pl.ds(start, piece)].astype(jnp.float32)
        source = jnp.concatenate([first, body], axis=1)
        for row in range(rows):
            spread = jnp.broadcast_to(source[row : row + 1, :], (FINE, LANES + piece))
            rolled = pltpu.roll(spread, 0, 1, stride=1, stride_axis=0)
            shifted_ref[row * FINE : (row + 1) * FINE, pl.ds(start, piece)] = rolled[
                :, LANES:
            ].astype(jnp.bfloat16)
        copy_of(shifted_ref, kept_ref, sems, step, start, piece).start()
        return 0

    lax.fori_loop(0, width // piece, one_piece, 0)


def lay_taps(tap_rows, slot_rows, receivers, sets):
    lane = iota((LANES, LANES), 1)
    source = iota((LANES, LANES), 0)
    spread = jnp.concatenate(
        [
            jnp.where(source == part * DELAYS + coarse * FINE + (lane & (FINE - 1)), 1.0, 0.0)
            for coarse in range(COARSE)
            for part in range(2)
        ],
        axis=1,
    )
    wide = jnp.dot(tap_rows, spread.astype(jnp.bfloat16), preferred_element_type=jnp.float32)
    here = iota((1, LANES), 1) >> 4
    count = PER_RECV * receivers
    seen = [
        [slot_rows[k * receivers : (k + 1) * receivers, :] == half * 8 + here for half in range(2)]
        for k in range(PER_RECV)
    ]
    laid = []
    for which in range(sets):
        blocks = []
        for coarse in range(COARSE):
            for out_part in range(2):
                tiles = []
                for half in range(2):
                    for in_part in range(2):
                        tile = (coarse * 2 + (in_part ^ out_part)) * LANES
                        total = jnp.zeros((receivers, LANES), jnp.float32)
                        for k in range(PER_RECV):
                            top = which * count + k * receivers
                            total = jnp.where(
                                seen[k][half],
                                total + wide[top : top + receivers, tile : tile + LANES],
                                total,
                            )
                        tiles.append(-total if in_part == 1 and out_part == 0 else total)
                blocks.append(jnp.concatenate(tiles, axis=1))
        laid.append(jnp.concatenate(blocks, axis=0).astype(jnp.bfloat16))
    return laid


def lay_gains_kernel(tap_ref, slot_rows_ref, out_ref):
    receivers = slot_rows_ref.shape[0] // PER_RECV
    high, low = lay_taps(tap_ref[...], slot_rows_ref[...], receivers, 2)
    rows = high.shape[0]
    out_ref[0:rows, :] = high
    out_ref[rows:, :] = low


def lay_gains(taps, slot_rows):
    vmem = pl.BlockSpec(memory_space=pltpu.VMEM)
    receivers = slot_rows.shape[0] // PER_RECV
    return pl.pallas_call(
        lay_gains_kernel,
        out_shape=jax.ShapeDtypeStruct((4 * COARSE * receivers, 32 * FINE), jnp.bfloat16),
        in_specs=[vmem, vmem],
        out_specs=vmem,
        compiler_params=pltpu.CompilerParams(vmem_limit_bytes=16 * 2**20),
        cost_estimate=pl.CostEstimate(flops=10**9, bytes_accessed=10**6, transcendentals=0),
        name="lay_gains",
    )(taps, slot_rows)


def coarse_sum(spread):
    rows = spread.shape[0] // COARSE
    total = spread[:rows, LANES:]
    for coarse in range(1, COARSE):
        total = total + pltpu.roll(spread[coarse * rows : (coarse + 1) * rows], coarse * FINE, 1)[:, LANES:]
    return total


def moved_ahead(ahead, span):
    moved = [ahead[:, :span].astype(jnp.bfloat16)]
    for coarse in range(1, COARSE):
        moved.append(
            pltpu.roll(ahead, span + LANES - coarse * FINE, 1)[:, :span].astype(jnp.bfloat16)
        )
    return jnp.concatenate(moved, axis=0)


def by_lag(read, rows, store):
    lane = iota((1, LANES), 1)
    for block in range(2):

        def one_slot(j, _, block=block):
            total = jnp.zeros((rows, LANES), jnp.float32)
            for coarse in range(COARSE):
                real = read(coarse, 0, 2 * block) + read(coarse, 1, 2 * block + 1)
                imag = read(coarse, 1, 2 * block) - read(coarse, 0, 2 * block + 1)
                place = coarse * FINE + LANES - j * FINE
                real = pltpu.roll(real, place, 1)
                imag = pltpu.roll(imag, place + DELAYS, 1)
                total = jnp.where(lane >> 4 == coarse, real, total)
                total = jnp.where(lane >> 4 == COARSE + coarse, imag, total)
            store(block * 8 + j, total * (1.0 / 262144.0))
            return 0

        lax.fori_loop(0, 8, one_slot, 0)


def fetch_all(kept_ref, shifted, sems, step_size):
    width = kept_ref.shape[1]
    lead = width % step_size
    steps = width // step_size
    if lead:
        copy_of(kept_ref, shifted, sems, steps, 0, lead).start()
    for step in range(steps):
        copy_of(kept_ref, shifted, sems, step, lead + step * step_size, step_size).start()
    if lead:
        copy_of(kept_ref, shifted, sems, steps, 0, lead).wait()

    def arrive(step):
        copy_of(kept_ref, shifted, sems, step, lead + step * step_size, step_size).wait()

    return arrive


def receive_kernel(
    slot_ref, taps_ref, refs_ref, echo_ref,
    received_ref, parts_ref, kept_ref,
    shifted, signal, outer, flipped, tidy, picked, corr, sems,
):
    receivers = echo_ref.shape[0] // 2
    length = echo_ref.shape[1]
    width = length + LANES
    heard_rows = 2 * receivers
    rows = heard_rows + 32
    groups = COARSE * heard_rows
    build_shifted(refs_ref, shifted, kept_ref, sems)
    signal[:, 0:LANES] = jnp.zeros((rows, LANES), jnp.bfloat16)
    signal[heard_rows:rows, LANES:width] = refs_ref[:, LANES:width]
    signal[:, width : width + LANES] = jnp.zeros((rows, LANES), jnp.bfloat16)

    def direct(step, _):
        start = pl.multiple_of(step * PIECE, LANES)
        window = shifted[:, pl.ds(start, LANES + PIECE)]
        spread = jnp.dot(
            taps_ref[0:groups, :], window, preferred_element_type=jnp.float32
        ) + jnp.dot(taps_ref[groups:, :], window, preferred_element_type=jnp.float32)
        echo = echo_ref[:, pl.ds(start, PIECE)].astype(jnp.float32)
        heard = (echo + coarse_sum(spread)).astype(jnp.bfloat16)
        received_ref[:, pl.ds(start, PIECE)] = heard
        signal[0:heard_rows, pl.ds(pl.multiple_of(start + LANES, LANES), PIECE)] = heard
        return 0

    lax.fori_loop(0, length // PIECE, direct, 0)
    outer[...] = jnp.zeros(outer.shape, jnp.float32)

    def correlate(step, _):
        start = pl.multiple_of(step * SPAN, LANES)
        outer[...] += lax.dot_general(
            shifted[:, pl.ds(start, SPAN)],
            moved_ahead(signal[:, pl.ds(start, SPAN + LANES)].astype(jnp.float32), SPAN),
            (((1,), (1,)), ((), ())),
            preferred_element_type=jnp.float32,
        )
        return 0

    lax.fori_loop(0, width // SPAN, correlate, 0)
    flipped[...] = jnp.transpose(outer[...])

    def read(coarse, out_part, tile):
        cols = slice(tile * LANES, (tile + 1) * LANES)
        top = coarse * rows + receivers * out_part
        low = coarse * rows + heard_rows + 8 * out_part
        return jnp.concatenate(
            [
                flipped[top : top + receivers, cols],
                flipped[low : low + 8, cols],
                flipped[low + 16 : low + 24, cols],
            ],
            axis=0,
        )

    def store(slot, lags):
        tidy[pl.ds(pl.multiple_of(slot * receivers, receivers), receivers), :] = lags[:receivers]
        corr[pl.ds(pl.multiple_of(slot * 16, 16), 16), :] = lags[receivers:]

    by_lag(read, receivers + 16, store)

    def pick(row, _):
        for k in range(PER_RECV):
            chosen = slot_ref[row, k] * receivers + row
            picked[pl.ds(k * receivers + row, 1), :] = tidy[pl.ds(chosen, 1), :]
        return 0

    lax.fori_loop(0, receivers, pick, 0, unroll=4)
    low = iota((1, LANES), 1) < DELAYS
    for pair in range(PER_RECV // 2):
        even = picked[2 * pair * receivers : (2 * pair + 1) * receivers, :]
        odd = picked[(2 * pair + 1) * receivers : (2 * pair + 2) * receivers, :]
        parts_ref[:, pair * LANES : (pair + 1) * LANES] = jnp.where(
            low, even, pltpu.roll(odd, DELAYS, 1)
        )
        pair += PER_RECV // 2
        parts_ref[:, pair * LANES : (pair + 1) * LANES] = jnp.where(
            low, pltpu.roll(even, DELAYS, 1), odd
        )
    each = 256 // receivers
    for row in range(each):
        tile = PER_RECV + row
        parts_ref[:, tile * LANES : (tile + 1) * LANES] = corr[pl.ds(row, receivers, stride=each), :]

    def sent(step, _):
        copy_of(shifted, kept_ref, sems, step, step * SPAN, SPAN).wait()
        return 0

    lax.fori_loop(0, width // SPAN, sent, 0)


def receive(slot, taps, refs, echoes):
    rows, length = echoes.shape
    receivers = rows // 2
    width = length + LANES
    smem = pl.BlockSpec(memory_space=pltpu.SMEM)
    vmem = pl.BlockSpec(memory_space=pltpu.VMEM)
    products = COARSE * (rows + 32)
    return pl.pallas_call(
        receive_kernel,
        out_shape=(
            jax.ShapeDtypeStruct((rows, length), jnp.bfloat16),
            jax.ShapeDtypeStruct((receivers, PARTS), jnp.float32),
            jax.ShapeDtypeStruct((32 * FINE, width), jnp.bfloat16),
        ),
        in_specs=[smem, vmem, vmem, vmem],
        out_specs=(vmem, vmem, pl.BlockSpec(memory_space=pl.ANY)),
        scratch_shapes=[
            pltpu.VMEM((32 * FINE, width), jnp.bfloat16),
            pltpu.VMEM((rows + 32, width + LANES), jnp.bfloat16),
            pltpu.VMEM((32 * FINE, products), jnp.float32),
            pltpu.VMEM((products, 32 * FINE), jnp.float32),
            pltpu.VMEM((16 * receivers, LANES), jnp.float32),
            pltpu.VMEM((PER_RECV * receivers, LANES), jnp.float32),
            pltpu.VMEM((256, LANES), jnp.float32),
            pltpu.SemaphoreType.DMA((width // SPAN,)),
        ],
        compiler_params=pltpu.CompilerParams(vmem_limit_bytes=RECEIVE_VMEM),
        name="receive",
    )(slot, taps, refs, echoes)


def cancel_kernel(
    solved_ref, slot_rows_ref, kept_ref, received_ref, out_ref, weights_ref, taps, shifted, sems
):
    receivers = received_ref.shape[0] // 2
    length = received_ref.shape[1]
    arrive = fetch_all(kept_ref, shifted, sems, PIECE)
    whole = PER_RECV * DELAYS
    weights_ref[0] = solved_ref[:, :whole]
    weights_ref[1] = solved_ref[:, whole:]
    low = iota((1, LANES), 1) < DELAYS
    rows = []
    for pair in range(PER_RECV // 2):
        real = solved_ref[:, pair * LANES : (pair + 1) * LANES]
        imag = solved_ref[:, whole + pair * LANES : whole + (pair + 1) * LANES]
        rows.append(jnp.where(low, real, pltpu.roll(imag, DELAYS, 1)))
        rows.append(jnp.where(low, pltpu.roll(real, DELAYS, 1), imag))
    tap_rows = jnp.concatenate(rows, axis=0).astype(jnp.bfloat16)
    taps[...] = lay_taps(tap_rows, slot_rows_ref[...], receivers, 1)[0]
    piece = PIECE

    def project(step, _):
        start = pl.multiple_of(step * piece, LANES)
        arrive(step)
        spread = jnp.dot(
            taps[...], shifted[:, pl.ds(start, LANES + piece)], preferred_element_type=jnp.float32
        )
        received = received_ref[:, pl.ds(start, piece)].astype(jnp.float32)
        out_ref[:, pl.ds(start, piece)] = (received - coarse_sum(spread)).astype(jnp.bfloat16)
        return 0

    lax.fori_loop(0, length // piece, project, 0)


def cancel(solved, slot_rows, shifted, received):
    rows, length = received.shape
    whole = PER_RECV * DELAYS
    vmem = pl.BlockSpec(memory_space=pltpu.VMEM)
    return pl.pallas_call(
        cancel_kernel,
        out_shape=(
            jax.ShapeDtypeStruct((rows, length), jnp.bfloat16),
            jax.ShapeDtypeStruct((2, rows // 2, whole), jnp.float32),
        ),
        in_specs=[vmem, vmem, pl.BlockSpec(memory_space=pl.ANY), vmem],
        out_specs=(vmem, vmem),
        scratch_shapes=[
            pltpu.VMEM((COARSE * rows, 32 * FINE), jnp.bfloat16),
            pltpu.VMEM((32 * FINE, length + LANES), jnp.bfloat16),
            pltpu.SemaphoreType.DMA((length // PIECE + 1,)),
        ],
        compiler_params=pltpu.CompilerParams(vmem_limit_bytes=RECEIVE_VMEM),
        name="cancel",
    )(solved, slot_rows, shifted, received)


def times_i(packed):
    sign = jnp.where(iota((1, LANES), 1) < DELAYS, -1.0, 1.0)
    count = packed.shape[1] // LANES
    blocks = [
        pltpu.roll(packed[:, b * LANES : (b + 1) * LANES], DELAYS, 1) * sign for b in range(count)
    ]
    return blocks[0] if count == 1 else jnp.concatenate(blocks, axis=1)


def inverse(block):
    size = block.shape[0]
    lane = iota((1, LANES), 1)
    low = lane & (DELAYS - 1)
    sub = iota((size, 1), 0)
    sign = jnp.where(lane < DELAYS, -1.0, 1.0)

    def spread(column):
        return jnp.broadcast_to(block[:, column : column + 1], (size, LANES))

    for first in range(0, size, PANEL):
        col_re = [spread(first + t) for t in range(PANEL)]
        col_im = [spread(DELAYS + first + t) for t in range(PANEL)]
        rows = [block[first + t : first + t + 1, :] for t in range(PANEL)]
        turned_rows = [pltpu.roll(row, DELAYS, 1) * sign for row in rows]
        block = jnp.where((low >= first) & (low < first + PANEL), 0.0, block)
        for t in range(PANEL):
            p = first + t
            over = 1.0 / col_re[t][p : p + 1, :]
            row = jnp.where(lane == p, 1.0, jnp.where(lane == DELAYS + p, 0.0, rows[t])) * over
            turned = (
                jnp.where(lane == DELAYS + p, 1.0, jnp.where(lane == p, 0.0, turned_rows[t])) * over
            )
            for u in range(t + 1, PANEL):
                q = first + u
                below_re = col_re[t][q : q + 1, :]
                below_im = col_im[t][q : q + 1, :]
                fac_re = below_re * over
                fac_im = -below_im * over
                next_re = col_re[u] - col_re[t] * fac_re + col_im[t] * fac_im
                next_im = col_im[u] - col_re[t] * fac_im - col_im[t] * fac_re
                col_re[u] = jnp.where(sub == p, fac_re, next_re)
                col_im[u] = jnp.where(sub == p, fac_im, next_im)
                rows[u] = jnp.where(low == p, 0.0, rows[u]) - below_re * row - below_im * turned
                turned_rows[u] = (
                    jnp.where(low == p, 0.0, turned_rows[u]) - below_re * turned + below_im * row
                )
            later = (low > p) & (low < first + PANEL)
            row = jnp.where(later, 0.0, row)
            turned = jnp.where(later, 0.0, turned)
            block = block - col_re[t] * row - col_im[t] * turned
            block = jnp.where(sub == p, row, block)
    return block


def exact_dot(left, right):
    return jnp.dot(left, right, precision=HIGHEST, preferred_element_type=jnp.float32)


def solve_kernel(slot_ref, corr_ref, cross_ref, out_ref, system, pairs):
    count = PER_RECV
    size = DELAYS
    for k in range(count):
        for l in range(count):
            row = k * count + l
            ahead = slot_ref[k] * 16 + slot_ref[l]
            behind = slot_ref[l] * 16 + slot_ref[k]
            pairs[row : row + 1, 0:LANES] = corr_ref[pl.ds(ahead, 1), :]
            pairs[row : row + 1, LANES : 2 * LANES] = corr_ref[pl.ds(behind, 1), :]
    pairs[count * count :, :] = jnp.zeros((pairs.shape[0] - count * count, 2 * LANES), jnp.float32)
    src = iota((2 * LANES, 2 * LANES), 0)
    dst = iota((2 * LANES, 2 * LANES), 1)
    x = dst & (LANES - 1)
    imag = dst >> 7
    from_ahead = jnp.where(x > size, imag * size + LANES - x, jnp.where(x == 0, imag * size, -1))
    from_behind_lag = jnp.where((x > 0) & (x < size), LANES + imag * size + x, -1)
    order = jnp.where(src == from_ahead, 1.0, 0.0) + jnp.where(
        src == from_behind_lag, jnp.where(imag == 1, -1.0, 1.0), 0.0
    )
    circular = exact_dot(pairs[...], order)
    lane = iota((1, LANES), 1)
    sub = iota((size, 1), 0)
    for k in range(count):
        for l in range(count):
            row = k * count + l
            real = jnp.broadcast_to(circular[row : row + 1, 0:LANES], (size, LANES))
            imag_part = jnp.broadcast_to(circular[row : row + 1, LANES:], (size, LANES))
            real = pltpu.roll(real, 0, 1, stride=1, stride_axis=0)
            imag_part = pltpu.roll(imag_part, size, 1, stride=1, stride_axis=0)
            block = jnp.where(lane < size, real, imag_part)
            if k == l:
                block = block + jnp.where(lane == sub, loading, 0.0)
            system[k * size : (k + 1) * size, l * LANES : (l + 1) * LANES] = block
    unit = jnp.where(lane == sub, 1.0, 0.0)

    def eliminate(i, _):
        mine = pl.ds(pl.multiple_of(i * size, size), size)
        col = pl.ds(pl.multiple_of(i * LANES, LANES), LANES)
        over = inverse(system[mine, col])
        system[mine, col] = unit
        right = system[mine, :]
        scaled = exact_dot(over, jnp.concatenate([right, times_i(right)], axis=0))
        factors = system[:, col]
        system[:, col] = jnp.zeros((count * size, LANES), jnp.float32)
        both = jnp.concatenate([scaled, times_i(scaled)], axis=0)
        system[...] = system[...] - exact_dot(factors, both)
        system[mine, :] = scaled
        return 0

    lax.fori_loop(0, count, eliminate, 0)
    whole = count * size
    total = cross_ref[...]
    sides = jnp.concatenate(
        [total[:, :whole], total[:, whole:], jnp.zeros((6, whole), jnp.float32)], axis=0
    )
    found = exact_dot(sides, system[...])
    rows = []
    for k in range(count):
        by_real = found[0:1, k * LANES : (k + 1) * LANES]
        by_imag = found[1:2, k * LANES : (k + 1) * LANES]
        rows.append(jnp.where(lane < size, by_real, -by_real) + pltpu.roll(by_imag, size, 1))
    for pair in range(count // 2):
        even, odd = rows[2 * pair], rows[2 * pair + 1]
        real = jnp.where(lane < size, even, pltpu.roll(odd, size, 1))
        imag = jnp.where(lane < size, pltpu.roll(even, size, 1), odd)
        low, high = pair * LANES, whole + pair * LANES
        shape = (out_ref.shape[0], LANES)
        out_ref[:, low : low + LANES] = jnp.broadcast_to(real, shape)
        out_ref[:, high : high + LANES] = jnp.broadcast_to(imag, shape)


def solve(slot, corr, cross, peers):
    smem = pl.BlockSpec(memory_space=pltpu.SMEM)
    vmem = pl.BlockSpec(memory_space=pltpu.VMEM)
    size = PER_RECV * DELAYS
    return pl.pallas_call(
        solve_kernel,
        out_shape=jax.ShapeDtypeStruct((peers, PER_RECV * LANES), jnp.float32),
        in_specs=[smem, vmem, vmem],
        out_specs=vmem,
        scratch_shapes=[
            pltpu.VMEM((size, PER_RECV * LANES), jnp.float32),
            pltpu.VMEM((40, 2 * LANES), jnp.float32),
        ],
        compiler_params=pltpu.CompilerParams(vmem_limit_bytes=16 * 2**20),
        name="solve",
    )(slot, corr, cross)


def local(symbols, incidence, delays, gains, echoes):
    owned, length = symbols.shape
    chan_count = lax.axis_size("chan")
    chan_index = lax.axis_index("chan")
    tm_count = lax.axis_size("tm")
    tm_index = lax.axis_index("tm")
    recv_count = echoes.shape[1]
    own = remodulate(symbols).reshape(2 * owned, length)
    following = passed_along(own, "chan", -1)
    own_halo = from_behind(own[:, length - LANES :], "tm", 1)
    next_halo = passed_along(own_halo, "chan", -1)
    refs = jnp.concatenate(
        [
            jnp.concatenate([own_halo, own], axis=1),
            jnp.concatenate([next_halo, following], axis=1),
        ],
        axis=0,
    )
    owner_chan = incidence // owned
    slot = (owner_chan - chan_index) % chan_count * owned + incidence % owned
    slot_rows = jnp.broadcast_to(
        slot.T.reshape(PER_RECV * recv_count, 1), (PER_RECV * recv_count, LANES)
    )
    lag = jnp.arange(LANES, dtype=jnp.int32)
    gain_rows = jnp.where(
        lag < DELAYS,
        gains[0].T.reshape(PER_RECV * recv_count, 1),
        gains[1].T.reshape(PER_RECV * recv_count, 1),
    )
    gain_taps = jnp.where(
        delays.T.reshape(PER_RECV * recv_count, 1) == (lag & (DELAYS - 1)), gain_rows, 0.0
    )
    tap_high = lax.reduce_precision(gain_taps, 8, 7)
    tap_low = (gain_taps - tap_high).astype(jnp.bfloat16)
    gain_rows = jnp.concatenate([tap_high.astype(jnp.bfloat16), tap_low], axis=0)
    laid = lay_gains(gain_rows, slot_rows)
    received, parts, shifted = receive(slot, laid, refs, echoes.reshape(2 * recv_count, length))
    share = recv_count // tm_count
    corr_share = 256 * LANES // tm_count
    parts = jnp.sum(lax.all_to_all(parts, "tm", 0, 0, tiled=True), axis=0, keepdims=True)
    my_cross = parts[:, : PER_RECV * LANES]
    my_corr = jnp.broadcast_to(parts[:, PER_RECV * LANES :], (tm_count, corr_share))
    corr = lax.all_to_all(my_corr, "tm", 0, 0, tiled=True).reshape(256, LANES)
    my_slot = lax.dynamic_slice_in_dim(slot, tm_index * share, share, 0).reshape(PER_RECV)
    mine = solve(my_slot, corr, my_cross, tm_count)
    solved = lax.all_to_all(mine, "tm", 0, 0, tiled=True)
    cancelled, weights = cancel(solved, slot_rows, shifted, received)
    return (cancelled.reshape(2, recv_count, length), weights)


def solution(mesh):
    in_specs = (
        P("chan", "tm"),
        P("chan", None),
        P("chan", None),
        P(None, "chan", None),
        P(None, "chan", "tm"),
    )
    out_specs = (P(None, "chan", "tm"), P(None, "chan", None))
    return jax.shard_map(local, mesh=mesh, in_specs=in_specs, out_specs=out_specs, check_vma=False)
```

```python
import math

import jax
import jax.numpy as jnp
import numpy as np
from jax import lax
from jax.experimental import pallas as pl
from jax.experimental.pallas import tpu as pltpu
from jax.sharding import PartitionSpec as P

ACTIVE = 6817
DELAYS = 64
PER_RECV = 6
LANES = 128
FINE = 16
COARSE = DELAYS // FINE
PARTS = PER_RECV * LANES + 1024
PANEL = 4
SPAN = 1664
PIECE = 2048
RECEIVE_VMEM = 56 * 2**20


loading = 0.1
HIGHEST = lax.Precision.HIGHEST


def passed_along(array, axis, by):
    peers = lax.axis_size(axis)
    return lax.ppermute(array, axis, [(i, (i + by) % peers) for i in range(peers)])


def from_behind(block, axis, distance):
    devices = range(lax.axis_size(axis))
    route = [(i - distance, i) for i in devices if i - distance in devices]
    return lax.ppermute(block, axis, route)


def parts_of(table, count):
    parts = []
    for _ in range(count):
        part = table.astype(jnp.bfloat16)
        parts.append(part)
        table = table - part.astype(np.float64)
    return parts


def wave_tables(length):
    tiles = length // LANES
    turn = 2.0 * np.pi / tiles

    def real_form(angle):
        return np.block([[np.cos(angle), -np.sin(angle)], [np.sin(angle), np.cos(angle)]])

    q = np.arange(tiles)
    v = np.arange(LANES)
    first = real_form(turn * ((q[:, None] * q[None, :]) % tiles))
    second = real_form(turn * ((q[:, None] * v[None, :]) % tiles))
    angle = 2.0 * np.pi / length * (v[:, None] * v[None, :])
    size = (1 - 2 * (v % 2))[:, None] / math.sqrt(ACTIVE * 42.0)
    between = np.stack([np.cos(angle) * size, np.sin(angle) * size]).astype(np.float32)
    high, low = parts_of(second, 2)
    return (
        np.concatenate(parts_of(first, 3), axis=1),
        np.concatenate([low, high, high], axis=1),
        between,
    )


def remodulate_kernel(symbols_ref, first_ref, second_ref, between_ref, out_ref, points, samples):
    emitters, length = symbols_ref.shape
    tiles = length // LANES
    for q in range(tiles):
        cols = slice(q * LANES, (q + 1) * LANES)
        symbol = symbols_ref[:, cols].astype(jnp.float32)
        column = jnp.floor(symbol * 0.125)
        tone = iota((1, LANES), 1) + (q * LANES - length // 2)
        used = (tone <= (ACTIVE - 1) // 2) & (tone >= -((ACTIVE - 1) // 2))
        rows = slice(q * emitters, (q + 1) * emitters)
        points[0, rows, :] = jnp.where(used, 2.0 * (symbol - 8.0 * column) - 7.0, 0.0)
        points[1, rows, :] = jnp.where(used, 2.0 * column - 7.0, 0.0)
    every = [pl.ds(n, tiles, stride=emitters) for n in range(emitters)]
    grid = jnp.concatenate(
        [
            jnp.concatenate([points[part, rows, :] for rows in every], axis=1).astype(jnp.bfloat16)
            for part in range(2)
        ],
        axis=0,
    )
    partial = jnp.dot(
        first_ref[...], jnp.concatenate([grid] * 3, axis=0), preferred_element_type=jnp.float32
    )
    turned = []
    for n in range(emitters):
        cols = slice(n * LANES, (n + 1) * LANES)
        real = jnp.concatenate([partial[:tiles, cols]] * 2, axis=0)
        imag = jnp.concatenate([partial[tiles:, cols]] * 2, axis=0)
        turned.append(
            jnp.concatenate(
                [
                    real * between_ref[0] - imag * between_ref[1],
                    real * between_ref[1] + imag * between_ref[0],
                ],
                axis=1,
            )
        )
    turned = jnp.concatenate(turned, axis=0)
    high = turned.astype(jnp.bfloat16)
    low = (turned - high.astype(jnp.float32)).astype(jnp.bfloat16)
    wave = lax.dot_general(
        second_ref[...],
        jnp.concatenate([high, low, high], axis=1),
        (((1,), (1,)), ((), ())),
        preferred_element_type=jnp.float32,
    )
    for part in range(2):
        for n in range(emitters):
            samples[part, every[n], :] = wave[
                part * tiles : (part + 1) * tiles, n * LANES : (n + 1) * LANES
            ]
    for q in range(tiles):
        rows = slice(q * emitters, (q + 1) * emitters)
        out_ref[:, q * LANES : (q + 1) * LANES] = jnp.concatenate(
            [samples[0, rows, :], samples[1, rows, :]], axis=0
        ).astype(jnp.bfloat16)


def remodulate(symbols):
    emitters, length = symbols.shape
    vmem = pl.BlockSpec(memory_space=pltpu.VMEM)
    first, second, between = (jnp.asarray(table) for table in wave_tables(length))
    return pl.pallas_call(
        remodulate_kernel,
        out_shape=jax.ShapeDtypeStruct((2 * emitters, length), jnp.bfloat16),
        in_specs=[vmem] * 4,
        out_specs=vmem,
        scratch_shapes=[
            pltpu.VMEM((2, emitters * length // LANES, LANES), jnp.float32),
            pltpu.VMEM((2, emitters * length // LANES, LANES), jnp.float32),
        ],
        compiler_params=pltpu.CompilerParams(vmem_limit_bytes=24 * 2**20),
        cost_estimate=pl.CostEstimate(flops=2 * 10**9, bytes_accessed=10**6, transcendentals=0),
        name="remodulate",
    )(symbols, first, second, between)


def iota(shape, axis):
    return lax.broadcasted_iota(jnp.int32, shape, axis)


def copy_of(source, target, sems, step, start, size):
    cols = pl.ds(pl.multiple_of(start, LANES), size)
    return pltpu.make_async_copy(source.at[:, cols], target.at[:, cols], sems.at[step])


def build_shifted(ref_ref, shifted_ref, kept_ref, sems):
    rows, width = ref_ref.shape
    piece = SPAN

    def one_piece(step, _):
        start = pl.multiple_of(step * piece, LANES)
        before = pl.multiple_of(jnp.maximum(start - LANES, 0), LANES)
        first = ref_ref[:, pl.ds(before, LANES)].astype(jnp.float32)
        body = ref_ref[:, pl.ds(start, piece)].astype(jnp.float32)
        source = jnp.concatenate([first, body], axis=1)
        for row in range(rows):
            spread = jnp.broadcast_to(source[row : row + 1, :], (FINE, LANES + piece))
            rolled = pltpu.roll(spread, 0, 1, stride=1, stride_axis=0)
            shifted_ref[row * FINE : (row + 1) * FINE, pl.ds(start, piece)] = rolled[
                :, LANES:
            ].astype(jnp.bfloat16)
        copy_of(shifted_ref, kept_ref, sems, step, start, piece).start()
        return 0

    lax.fori_loop(0, width // piece, one_piece, 0)


def lay_taps(tap_rows, slot_rows, receivers, sets):
    lane = iota((LANES, LANES), 1)
    source = iota((LANES, LANES), 0)
    spread = jnp.concatenate(
        [
            jnp.where(source == part * DELAYS + coarse * FINE + (lane & (FINE - 1)), 1.0, 0.0)
            for coarse in range(COARSE)
            for part in range(2)
        ],
        axis=1,
    )
    wide = jnp.dot(tap_rows, spread.astype(jnp.bfloat16), preferred_element_type=jnp.float32)
    here = iota((1, LANES), 1) >> 4
    count = PER_RECV * receivers
    seen = [
        [slot_rows[k * receivers : (k + 1) * receivers, :] == half * 8 + here for half in range(2)]
        for k in range(PER_RECV)
    ]
    laid = []
    for which in range(sets):
        blocks = []
        for coarse in range(COARSE):
            for out_part in range(2):
                tiles = []
                for half in range(2):
                    for in_part in range(2):
                        tile = (coarse * 2 + (in_part ^ out_part)) * LANES
                        total = jnp.zeros((receivers, LANES), jnp.float32)
                        for k in range(PER_RECV):
                            top = which * count + k * receivers
                            total = jnp.where(
                                seen[k][half],
                                total + wide[top : top + receivers, tile : tile + LANES],
                                total,
                            )
                        tiles.append(-total if in_part == 1 and out_part == 0 else total)
                blocks.append(jnp.concatenate(tiles, axis=1))
        laid.append(jnp.concatenate(blocks, axis=0).astype(jnp.bfloat16))
    return laid


def lay_gains_kernel(tap_ref, slot_rows_ref, out_ref):
    receivers = slot_rows_ref.shape[0] // PER_RECV
    high, low = lay_taps(tap_ref[...], slot_rows_ref[...], receivers, 2)
    rows = high.shape[0]
    out_ref[0:rows, :] = high
    out_ref[rows:, :] = low


def lay_gains(taps, slot_rows):
    vmem = pl.BlockSpec(memory_space=pltpu.VMEM)
    receivers = slot_rows.shape[0] // PER_RECV
    return pl.pallas_call(
        lay_gains_kernel,
        out_shape=jax.ShapeDtypeStruct((4 * COARSE * receivers, 32 * FINE), jnp.bfloat16),
        in_specs=[vmem, vmem],
        out_specs=vmem,
        compiler_params=pltpu.CompilerParams(vmem_limit_bytes=16 * 2**20),
        cost_estimate=pl.CostEstimate(flops=10**9, bytes_accessed=10**6, transcendentals=0),
        name="lay_gains",
    )(taps, slot_rows)


def coarse_sum(spread):
    rows = spread.shape[0] // COARSE
    total = spread[:rows, LANES:]
    for coarse in range(1, COARSE):
        total = total + pltpu.roll(spread[coarse * rows : (coarse + 1) * rows], coarse * FINE, 1)[:, LANES:]
    return total


def moved_ahead(ahead, span):
    moved = [ahead[:, :span].astype(jnp.bfloat16)]
    for coarse in range(1, COARSE):
        moved.append(
            pltpu.roll(ahead, span + LANES - coarse * FINE, 1)[:, :span].astype(jnp.bfloat16)
        )
    return jnp.concatenate(moved, axis=0)


def by_lag(read, rows, store):
    lane = iota((1, LANES), 1)
    for block in range(2):

        def one_slot(j, _, block=block):
            total = jnp.zeros((rows, LANES), jnp.float32)
            for coarse in range(COARSE):
                real = read(coarse, 0, 2 * block) + read(coarse, 1, 2 * block + 1)
                imag = read(coarse, 1, 2 * block) - read(coarse, 0, 2 * block + 1)
                place = coarse * FINE + LANES - j * FINE
                real = pltpu.roll(real, place, 1)
                imag = pltpu.roll(imag, place + DELAYS, 1)
                total = jnp.where(lane >> 4 == coarse, real, total)
                total = jnp.where(lane >> 4 == COARSE + coarse, imag, total)
            store(block * 8 + j, total * (1.0 / 262144.0))
            return 0

        lax.fori_loop(0, 8, one_slot, 0)


def fetch_all(kept_ref, shifted, sems, step_size):
    width = kept_ref.shape[1]
    lead = width % step_size
    steps = width // step_size
    if lead:
        copy_of(kept_ref, shifted, sems, steps, 0, lead).start()
    for step in range(steps):
        copy_of(kept_ref, shifted, sems, step, lead + step * step_size, step_size).start()
    if lead:
        copy_of(kept_ref, shifted, sems, steps, 0, lead).wait()

    def arrive(step):
        copy_of(kept_ref, shifted, sems, step, lead + step * step_size, step_size).wait()

    return arrive


def receive_kernel(
    slot_ref, taps_ref, refs_ref, echo_ref,
    received_ref, parts_ref, kept_ref,
    shifted, signal, outer, flipped, tidy, picked, corr, sems,
):
    receivers = echo_ref.shape[0] // 2
    length = echo_ref.shape[1]
    width = length + LANES
    heard_rows = 2 * receivers
    rows = heard_rows + 32
    groups = COARSE * heard_rows
    build_shifted(refs_ref, shifted, kept_ref, sems)
    signal[:, 0:LANES] = jnp.zeros((rows, LANES), jnp.bfloat16)
    signal[heard_rows:rows, LANES:width] = refs_ref[:, LANES:width]
    signal[:, width : width + LANES] = jnp.zeros((rows, LANES), jnp.bfloat16)

    def direct(step, _):
        start = pl.multiple_of(step * PIECE, LANES)
        window = shifted[:, pl.ds(start, LANES + PIECE)]
        spread = jnp.dot(
            taps_ref[0:groups, :], window, preferred_element_type=jnp.float32
        ) + jnp.dot(taps_ref[groups:, :], window, preferred_element_type=jnp.float32)
        echo = echo_ref[:, pl.ds(start, PIECE)].astype(jnp.float32)
        heard = (echo + coarse_sum(spread)).astype(jnp.bfloat16)
        received_ref[:, pl.ds(start, PIECE)] = heard
        signal[0:heard_rows, pl.ds(pl.multiple_of(start + LANES, LANES), PIECE)] = heard
        return 0

    lax.fori_loop(0, length // PIECE, direct, 0)
    outer[...] = jnp.zeros(outer.shape, jnp.float32)

    def correlate(step, _):
        start = pl.multiple_of(step * SPAN, LANES)
        outer[...] += lax.dot_general(
            shifted[:, pl.ds(start, SPAN)],
            moved_ahead(signal[:, pl.ds(start, SPAN + LANES)].astype(jnp.float32), SPAN),
            (((1,), (1,)), ((), ())),
            preferred_element_type=jnp.float32,
        )
        return 0

    lax.fori_loop(0, width // SPAN, correlate, 0)
    flipped[...] = jnp.transpose(outer[...])

    def read(coarse, out_part, tile):
        cols = slice(tile * LANES, (tile + 1) * LANES)
        top = coarse * rows + receivers * out_part
        low = coarse * rows + heard_rows + 8 * out_part
        return jnp.concatenate(
            [
                flipped[top : top + receivers, cols],
                flipped[low : low + 8, cols],
                flipped[low + 16 : low + 24, cols],
            ],
            axis=0,
        )

    def store(slot, lags):
        tidy[pl.ds(pl.multiple_of(slot * receivers, receivers), receivers), :] = lags[:receivers]
        corr[pl.ds(pl.multiple_of(slot * 16, 16), 16), :] = lags[receivers:]

    by_lag(read, receivers + 16, store)

    def pick(row, _):
        for k in range(PER_RECV):
            chosen = slot_ref[row, k] * receivers + row
            picked[pl.ds(k * receivers + row, 1), :] = tidy[pl.ds(chosen, 1), :]
        return 0

    lax.fori_loop(0, receivers, pick, 0, unroll=4)
    low = iota((1, LANES), 1) < DELAYS
    for pair in range(PER_RECV // 2):
        even = picked[2 * pair * receivers : (2 * pair + 1) * receivers, :]
        odd = picked[(2 * pair + 1) * receivers : (2 * pair + 2) * receivers, :]
        parts_ref[:, pair * LANES : (pair + 1) * LANES] = jnp.where(
            low, even, pltpu.roll(odd, DELAYS, 1)
        )
        pair += PER_RECV // 2
        parts_ref[:, pair * LANES : (pair + 1) * LANES] = jnp.where(
            low, pltpu.roll(even, DELAYS, 1), odd
        )
    each = 256 // receivers
    for row in range(each):
        tile = PER_RECV + row
        parts_ref[:, tile * LANES : (tile + 1) * LANES] = corr[pl.ds(row, receivers, stride=each), :]

    def sent(step, _):
        copy_of(shifted, kept_ref, sems, step, step * SPAN, SPAN).wait()
        return 0

    lax.fori_loop(0, width // SPAN, sent, 0)


def receive(slot, taps, refs, echoes):
    rows, length = echoes.shape
    receivers = rows // 2
    width = length + LANES
    smem = pl.BlockSpec(memory_space=pltpu.SMEM)
    vmem = pl.BlockSpec(memory_space=pltpu.VMEM)
    products = COARSE * (rows + 32)
    return pl.pallas_call(
        receive_kernel,
        out_shape=(
            jax.ShapeDtypeStruct((rows, length), jnp.bfloat16),
            jax.ShapeDtypeStruct((receivers, PARTS), jnp.float32),
            jax.ShapeDtypeStruct((32 * FINE, width), jnp.bfloat16),
        ),
        in_specs=[smem, vmem, vmem, vmem],
        out_specs=(vmem, vmem, pl.BlockSpec(memory_space=pl.ANY)),
        scratch_shapes=[
            pltpu.VMEM((32 * FINE, width), jnp.bfloat16),
            pltpu.VMEM((rows + 32, width + LANES), jnp.bfloat16),
            pltpu.VMEM((32 * FINE, products), jnp.float32),
            pltpu.VMEM((products, 32 * FINE), jnp.float32),
            pltpu.VMEM((16 * receivers, LANES), jnp.float32),
            pltpu.VMEM((PER_RECV * receivers, LANES), jnp.float32),
            pltpu.VMEM((256, LANES), jnp.float32),
            pltpu.SemaphoreType.DMA((width // SPAN,)),
        ],
        compiler_params=pltpu.CompilerParams(vmem_limit_bytes=RECEIVE_VMEM),
        name="receive",
    )(slot, taps, refs, echoes)


def cancel_kernel(
    solved_ref, slot_rows_ref, kept_ref, received_ref, out_ref, weights_ref, taps, shifted, sems
):
    receivers = received_ref.shape[0] // 2
    length = received_ref.shape[1]
    arrive = fetch_all(kept_ref, shifted, sems, PIECE)
    whole = PER_RECV * DELAYS
    weights_ref[0] = solved_ref[:, :whole]
    weights_ref[1] = solved_ref[:, whole:]
    low = iota((1, LANES), 1) < DELAYS
    rows = []
    for pair in range(PER_RECV // 2):
        real = solved_ref[:, pair * LANES : (pair + 1) * LANES]
        imag = solved_ref[:, whole + pair * LANES : whole + (pair + 1) * LANES]
        rows.append(jnp.where(low, real, pltpu.roll(imag, DELAYS, 1)))
        rows.append(jnp.where(low, pltpu.roll(real, DELAYS, 1), imag))
    tap_rows = jnp.concatenate(rows, axis=0).astype(jnp.bfloat16)
    taps[...] = lay_taps(tap_rows, slot_rows_ref[...], receivers, 1)[0]
    piece = PIECE

    def project(step, _):
        start = pl.multiple_of(step * piece, LANES)
        arrive(step)
        spread = jnp.dot(
            taps[...], shifted[:, pl.ds(start, LANES + piece)], preferred_element_type=jnp.float32
        )
        received = received_ref[:, pl.ds(start, piece)].astype(jnp.float32)
        out_ref[:, pl.ds(start, piece)] = (received - coarse_sum(spread)).astype(jnp.bfloat16)
        return 0

    lax.fori_loop(0, length // piece, project, 0)


def cancel(solved, slot_rows, shifted, received):
    rows, length = received.shape
    whole = PER_RECV * DELAYS
    vmem = pl.BlockSpec(memory_space=pltpu.VMEM)
    return pl.pallas_call(
        cancel_kernel,
        out_shape=(
            jax.ShapeDtypeStruct((rows, length), jnp.bfloat16),
            jax.ShapeDtypeStruct((2, rows // 2, whole), jnp.float32),
        ),
        in_specs=[vmem, vmem, pl.BlockSpec(memory_space=pl.ANY), vmem],
        out_specs=(vmem, vmem),
        scratch_shapes=[
            pltpu.VMEM((COARSE * rows, 32 * FINE), jnp.bfloat16),
            pltpu.VMEM((32 * FINE, length + LANES), jnp.bfloat16),
            pltpu.SemaphoreType.DMA((length // PIECE + 1,)),
        ],
        compiler_params=pltpu.CompilerParams(vmem_limit_bytes=RECEIVE_VMEM),
        name="cancel",
    )(solved, slot_rows, shifted, received)


def times_i(packed):
    sign = jnp.where(iota((1, LANES), 1) < DELAYS, -1.0, 1.0)
    count = packed.shape[1] // LANES
    blocks = [
        pltpu.roll(packed[:, b * LANES : (b + 1) * LANES], DELAYS, 1) * sign for b in range(count)
    ]
    return blocks[0] if count == 1 else jnp.concatenate(blocks, axis=1)


def inverse(block):
    size = block.shape[0]
    lane = iota((1, LANES), 1)
    low = lane & (DELAYS - 1)
    sub = iota((size, 1), 0)
    sign = jnp.where(lane < DELAYS, -1.0, 1.0)

    def spread(column):
        return jnp.broadcast_to(block[:, column : column + 1], (size, LANES))

    for first in range(0, size, PANEL):
        col_re = [spread(first + t) for t in range(PANEL)]
        col_im = [spread(DELAYS + first + t) for t in range(PANEL)]
        rows = [block[first + t : first + t + 1, :] for t in range(PANEL)]
        turned_rows = [pltpu.roll(row, DELAYS, 1) * sign for row in rows]
        block = jnp.where((low >= first) & (low < first + PANEL), 0.0, block)
        for t in range(PANEL):
            p = first + t
            over = 1.0 / col_re[t][p : p + 1, :]
            row = jnp.where(lane == p, 1.0, jnp.where(lane == DELAYS + p, 0.0, rows[t])) * over
            turned = (
                jnp.where(lane == DELAYS + p, 1.0, jnp.where(lane == p, 0.0, turned_rows[t])) * over
            )
            for u in range(t + 1, PANEL):
                q = first + u
                below_re = col_re[t][q : q + 1, :]
                below_im = col_im[t][q : q + 1, :]
                fac_re = below_re * over
                fac_im = -below_im * over
                next_re = col_re[u] - col_re[t] * fac_re + col_im[t] * fac_im
                next_im = col_im[u] - col_re[t] * fac_im - col_im[t] * fac_re
                col_re[u] = jnp.where(sub == p, fac_re, next_re)
                col_im[u] = jnp.where(sub == p, fac_im, next_im)
                rows[u] = jnp.where(low == p, 0.0, rows[u]) - below_re * row - below_im * turned
                turned_rows[u] = (
                    jnp.where(low == p, 0.0, turned_rows[u]) - below_re * turned + below_im * row
                )
            later = (low > p) & (low < first + PANEL)
            row = jnp.where(later, 0.0, row)
            turned = jnp.where(later, 0.0, turned)
            block = block - col_re[t] * row - col_im[t] * turned
            block = jnp.where(sub == p, row, block)
    return block


def exact_dot(left, right):
    return jnp.dot(left, right, precision=HIGHEST, preferred_element_type=jnp.float32)


def three_parts(array):
    high = array.astype(jnp.bfloat16)
    rest = array - high.astype(jnp.float32)
    middle = rest.astype(jnp.bfloat16)
    return high, middle, (rest - middle.astype(jnp.float32)).astype(jnp.bfloat16)


def deep_dot(left, right):
    lh, lm, ll = three_parts(left)
    rh, rm, rl = three_parts(right)
    return jnp.dot(
        jnp.concatenate([ll, lh, lm, lm, lh, lh], axis=1),
        jnp.concatenate([rh, rl, rm, rh, rm, rh], axis=0),
        preferred_element_type=jnp.float32,
    )


def solve_kernel(slot_ref, corr_ref, cross_ref, out_ref, system, pairs):
    count = PER_RECV
    size = DELAYS
    for k in range(count):
        for l in range(count):
            row = k * count + l
            ahead = slot_ref[k] * 16 + slot_ref[l]
            behind = slot_ref[l] * 16 + slot_ref[k]
            pairs[row : row + 1, 0:LANES] = corr_ref[pl.ds(ahead, 1), :]
            pairs[row : row + 1, LANES : 2 * LANES] = corr_ref[pl.ds(behind, 1), :]
    pairs[count * count :, :] = jnp.zeros((pairs.shape[0] - count * count, 2 * LANES), jnp.float32)
    src = iota((2 * LANES, 2 * LANES), 0)
    dst = iota((2 * LANES, 2 * LANES), 1)
    x = dst & (LANES - 1)
    imag = dst >> 7
    from_ahead = jnp.where(x > size, imag * size + LANES - x, jnp.where(x == 0, imag * size, -1))
    from_behind_lag = jnp.where((x > 0) & (x < size), LANES + imag * size + x, -1)
    order = jnp.where(src == from_ahead, 1.0, 0.0) + jnp.where(
        src == from_behind_lag, jnp.where(imag == 1, -1.0, 1.0), 0.0
    )
    circular = exact_dot(pairs[...], order)
    lane = iota((1, LANES), 1)
    sub = iota((size, 1), 0)
    for k in range(count):
        for l in range(count):
            row = k * count + l
            real = jnp.broadcast_to(circular[row : row + 1, 0:LANES], (size, LANES))
            imag_part = jnp.broadcast_to(circular[row : row + 1, LANES:], (size, LANES))
            real = pltpu.roll(real, 0, 1, stride=1, stride_axis=0)
            imag_part = pltpu.roll(imag_part, size, 1, stride=1, stride_axis=0)
            block = jnp.where(lane < size, real, imag_part)
            if k == l:
                block = block + jnp.where(lane == sub, loading, 0.0)
            system[k * size : (k + 1) * size, l * LANES : (l + 1) * LANES] = block
    unit = jnp.where(lane == sub, 1.0, 0.0)

    def eliminate(i, _):
        mine = pl.ds(pl.multiple_of(i * size, size), size)
        col = pl.ds(pl.multiple_of(i * LANES, LANES), LANES)
        over = inverse(system[mine, col])
        system[mine, col] = unit
        right = system[mine, :]
        scaled = deep_dot(over, jnp.concatenate([right, times_i(right)], axis=0))
        factors = system[:, col]
        system[:, col] = jnp.zeros((count * size, LANES), jnp.float32)
        both = jnp.concatenate([scaled, times_i(scaled)], axis=0)
        system[...] = system[...] - deep_dot(factors, both)
        system[mine, :] = scaled
        return 0

    lax.fori_loop(0, count, eliminate, 0)
    whole = count * size
    total = cross_ref[...]
    sides = jnp.concatenate(
        [total[:, :whole], total[:, whole:], jnp.zeros((6, whole), jnp.float32)], axis=0
    )
    found = exact_dot(sides, system[...])
    rows = []
    for k in range(count):
        by_real = found[0:1, k * LANES : (k + 1) * LANES]
        by_imag = found[1:2, k * LANES : (k + 1) * LANES]
        rows.append(jnp.where(lane < size, by_real, -by_real) + pltpu.roll(by_imag, size, 1))
    for pair in range(count // 2):
        even, odd = rows[2 * pair], rows[2 * pair + 1]
        real = jnp.where(lane < size, even, pltpu.roll(odd, size, 1))
        imag = jnp.where(lane < size, pltpu.roll(even, size, 1), odd)
        low, high = pair * LANES, whole + pair * LANES
        shape = (out_ref.shape[0], LANES)
        out_ref[:, low : low + LANES] = jnp.broadcast_to(real, shape)
        out_ref[:, high : high + LANES] = jnp.broadcast_to(imag, shape)


def solve(slot, corr, cross, peers):
    smem = pl.BlockSpec(memory_space=pltpu.SMEM)
    vmem = pl.BlockSpec(memory_space=pltpu.VMEM)
    size = PER_RECV * DELAYS
    return pl.pallas_call(
        solve_kernel,
        out_shape=jax.ShapeDtypeStruct((peers, PER_RECV * LANES), jnp.float32),
        in_specs=[smem, vmem, vmem],
        out_specs=vmem,
        scratch_shapes=[
            pltpu.VMEM((size, PER_RECV * LANES), jnp.float32),
            pltpu.VMEM((40, 2 * LANES), jnp.float32),
        ],
        compiler_params=pltpu.CompilerParams(vmem_limit_bytes=16 * 2**20),
        name="solve",
    )(slot, corr, cross)


def local(symbols, incidence, delays, gains, echoes):
    owned, length = symbols.shape
    chan_count = lax.axis_size("chan")
    chan_index = lax.axis_index("chan")
    tm_count = lax.axis_size("tm")
    tm_index = lax.axis_index("tm")
    recv_count = echoes.shape[1]
    sent = symbols.astype(jnp.bfloat16)
    next_symbols = passed_along(sent, "chan", -1)
    own = remodulate(sent)
    own_halo = from_behind(own[:, length - LANES :], "tm", 1)
    next_halo = passed_along(own_halo, "chan", -1)
    following = remodulate(next_symbols)
    refs = jnp.concatenate(
        [
            jnp.concatenate([own_halo, own], axis=1),
            jnp.concatenate([next_halo, following], axis=1),
        ],
        axis=0,
    )
    owner_chan = incidence // owned
    slot = (owner_chan - chan_index) % chan_count * owned + incidence % owned
    slot_rows = jnp.broadcast_to(
        slot.T.reshape(PER_RECV * recv_count, 1), (PER_RECV * recv_count, LANES)
    )
    lag = jnp.arange(LANES, dtype=jnp.int32)
    gain_rows = jnp.where(
        lag < DELAYS,
        gains[0].T.reshape(PER_RECV * recv_count, 1),
        gains[1].T.reshape(PER_RECV * recv_count, 1),
    )
    gain_taps = jnp.where(
        delays.T.reshape(PER_RECV * recv_count, 1) == (lag & (DELAYS - 1)), gain_rows, 0.0
    )
    tap_high = lax.reduce_precision(gain_taps, 8, 7)
    tap_low = (gain_taps - tap_high).astype(jnp.bfloat16)
    gain_rows = jnp.concatenate([tap_high.astype(jnp.bfloat16), tap_low], axis=0)
    laid = lay_gains(gain_rows, slot_rows)
    received, parts, shifted = receive(slot, laid, refs, echoes.reshape(2 * recv_count, length))
    share = recv_count // tm_count
    corr_share = 256 * LANES // tm_count
    parts = jnp.sum(lax.all_to_all(parts, "tm", 0, 0, tiled=True), axis=0, keepdims=True)
    my_cross = parts[:, : PER_RECV * LANES]
    my_corr = jnp.broadcast_to(parts[:, PER_RECV * LANES :], (tm_count, corr_share))
    corr = lax.all_to_all(my_corr, "tm", 0, 0, tiled=True).reshape(256, LANES)
    my_slot = lax.dynamic_slice_in_dim(slot, tm_index * share, share, 0).reshape(PER_RECV)
    mine = solve(my_slot, corr, my_cross, tm_count)
    solved = lax.all_to_all(mine, "tm", 0, 0, tiled=True)
    cancelled, weights = cancel(solved, slot_rows, shifted, received)
    return (cancelled.reshape(2, recv_count, length), weights)


def solution(mesh):
    in_specs = (
        P("chan", "tm"),
        P("chan", None),
        P("chan", None),
        P(None, "chan", None),
        P(None, "chan", "tm"),
    )
    out_specs = (P(None, "chan", "tm"), P(None, "chan", None))
    return jax.shard_map(local, mesh=mesh, in_specs=in_specs, out_specs=out_specs, check_vma=False)
```

```python
import math

import jax
import jax.numpy as jnp
import numpy as np
from jax import lax
from jax.experimental import pallas as pl
from jax.experimental.pallas import tpu as pltpu
from jax.sharding import PartitionSpec as P

ACTIVE = 6817
DELAYS = 64
PER_RECV = 6
LANES = 128
FINE = 16
COARSE = DELAYS // FINE
PARTS = PER_RECV * LANES + 1024
PANEL = 4
SPAN = 1664
PIECE = 2048
RECEIVE_VMEM = 56 * 2**20


loading = 0.1
HIGHEST = lax.Precision.HIGHEST


def passed_along(array, axis, by):
    peers = lax.axis_size(axis)
    return lax.ppermute(array, axis, [(i, (i + by) % peers) for i in range(peers)])


def from_behind(block, axis, distance):
    devices = range(lax.axis_size(axis))
    route = [(i - distance, i) for i in devices if i - distance in devices]
    return lax.ppermute(block, axis, route)


def parts_of(table, count):
    parts = []
    for _ in range(count):
        part = table.astype(jnp.bfloat16).astype(np.float64)
        parts.append(part)
        table = table - part
    return parts


def wave_tables(length):
    tiles = length // LANES
    turn = 2.0 * np.pi / tiles

    def real_form(angle):
        return np.block([[np.cos(angle), -np.sin(angle)], [np.sin(angle), np.cos(angle)]])

    q = np.arange(tiles)
    v = np.arange(LANES)
    first = real_form(turn * ((q[:, None] * q[None, :]) % tiles))
    second = real_form(turn * ((q[:, None] * v[None, :]) % tiles))
    angle = 2.0 * np.pi / length * (v[:, None] * v[None, :])
    size = (1 - 2 * (v % 2))[:, None] / math.sqrt(ACTIVE * 42.0)
    high, low = parts_of(second, 2)
    return np.concatenate(
        [*parts_of(first, 3), low, high, high, np.cos(angle) * size, np.sin(angle) * size],
        axis=1,
        dtype=np.float32,
    )


def remodulate_kernel(own_ref, next_ref, table_ref, out_ref, points, samples):
    owned, length = own_ref.shape
    emitters = 2 * owned
    first = table_ref[:, 0 : 3 * LANES].astype(jnp.bfloat16)
    second = table_ref[:, 3 * LANES : 9 * LANES].astype(jnp.bfloat16)
    along = table_ref[:, 9 * LANES : 10 * LANES]
    across = table_ref[:, 10 * LANES :]
    tiles = length // LANES
    for q in range(tiles):
        cols = slice(q * LANES, (q + 1) * LANES)
        symbol = jnp.concatenate([own_ref[:, cols], next_ref[:, cols]], axis=0).astype(jnp.float32)
        column = jnp.floor(symbol * 0.125)
        tone = iota((1, LANES), 1) + (q * LANES - length // 2)
        used = (tone <= (ACTIVE - 1) // 2) & (tone >= -((ACTIVE - 1) // 2))
        rows = slice(q * emitters, (q + 1) * emitters)
        points[0, rows, :] = jnp.where(used, 2.0 * (symbol - 8.0 * column) - 7.0, 0.0)
        points[1, rows, :] = jnp.where(used, 2.0 * column - 7.0, 0.0)
    every = [pl.ds(n, tiles, stride=emitters) for n in range(emitters)]
    grid = jnp.concatenate(
        [
            jnp.concatenate([points[part, rows, :] for rows in every], axis=1).astype(jnp.bfloat16)
            for part in range(2)
        ],
        axis=0,
    )
    partial = jnp.dot(
        first, jnp.concatenate([grid] * 3, axis=0), preferred_element_type=jnp.float32
    )
    turned = []
    for n in range(emitters):
        cols = slice(n * LANES, (n + 1) * LANES)
        real = jnp.concatenate([partial[:tiles, cols]] * 2, axis=0)
        imag = jnp.concatenate([partial[tiles:, cols]] * 2, axis=0)
        turned.append(
            jnp.concatenate(
                [
                    real * along - imag * across,
                    real * across + imag * along,
                ],
                axis=1,
            )
        )
    turned = jnp.concatenate(turned, axis=0)
    high = turned.astype(jnp.bfloat16)
    low = (turned - high.astype(jnp.float32)).astype(jnp.bfloat16)
    wave = lax.dot_general(
        second,
        jnp.concatenate([high, low, high], axis=1),
        (((1,), (1,)), ((), ())),
        preferred_element_type=jnp.float32,
    )
    for part in range(2):
        for n in range(emitters):
            samples[part, every[n], :] = wave[
                part * tiles : (part + 1) * tiles, n * LANES : (n + 1) * LANES
            ]
    for q in range(tiles):
        out_ref[:, q * LANES : (q + 1) * LANES] = jnp.concatenate(
            [
                samples[part, q * emitters + side * owned : q * emitters + (side + 1) * owned, :]
                for side in range(2)
                for part in range(2)
            ],
            axis=0,
        ).astype(jnp.bfloat16)


def remodulate(own, following):
    owned, length = own.shape
    emitters = 2 * owned
    vmem = pl.BlockSpec(memory_space=pltpu.VMEM)
    return pl.pallas_call(
        remodulate_kernel,
        out_shape=jax.ShapeDtypeStruct((2 * emitters, length), jnp.bfloat16),
        in_specs=[vmem] * 3,
        out_specs=vmem,
        scratch_shapes=[
            pltpu.VMEM((2, emitters * length // LANES, LANES), jnp.float32),
            pltpu.VMEM((2, emitters * length // LANES, LANES), jnp.float32),
        ],
        compiler_params=pltpu.CompilerParams(vmem_limit_bytes=24 * 2**20),
        cost_estimate=pl.CostEstimate(flops=2 * 10**9, bytes_accessed=10**6, transcendentals=0),
        name="remodulate",
    )(own, following, jnp.asarray(wave_tables(length)))


def iota(shape, axis):
    return lax.broadcasted_iota(jnp.int32, shape, axis)


def copy_of(source, target, sems, step, start, size):
    cols = pl.ds(pl.multiple_of(start, LANES), size)
    return pltpu.make_async_copy(source.at[:, cols], target.at[:, cols], sems.at[step])


def build_shifted(ref_ref, shifted_ref, kept_ref, sems):
    rows, width = ref_ref.shape
    piece = SPAN

    def one_piece(step, _):
        start = pl.multiple_of(step * piece, LANES)
        before = pl.multiple_of(jnp.maximum(start - LANES, 0), LANES)
        first = ref_ref[:, pl.ds(before, LANES)].astype(jnp.float32)
        body = ref_ref[:, pl.ds(start, piece)].astype(jnp.float32)
        source = jnp.concatenate([first, body], axis=1)
        for row in range(rows):
            spread = jnp.broadcast_to(source[row : row + 1, :], (FINE, LANES + piece))
            rolled = pltpu.roll(spread, 0, 1, stride=1, stride_axis=0)
            shifted_ref[row * FINE : (row + 1) * FINE, pl.ds(start, piece)] = rolled[
                :, LANES:
            ].astype(jnp.bfloat16)
        copy_of(shifted_ref, kept_ref, sems, step, start, piece).start()
        return 0

    lax.fori_loop(0, width // piece, one_piece, 0)


def lay_taps(tap_rows, slot_rows, receivers, sets):
    lane = iota((LANES, LANES), 1)
    source = iota((LANES, LANES), 0)
    spread = jnp.concatenate(
        [
            jnp.where(source == part * DELAYS + coarse * FINE + (lane & (FINE - 1)), 1.0, 0.0)
            for coarse in range(COARSE)
            for part in range(2)
        ],
        axis=1,
    )
    wide = jnp.dot(tap_rows, spread.astype(jnp.bfloat16), preferred_element_type=jnp.float32)
    here = iota((1, LANES), 1) >> 4
    count = PER_RECV * receivers
    seen = [
        [slot_rows[k * receivers : (k + 1) * receivers, :] == half * 8 + here for half in range(2)]
        for k in range(PER_RECV)
    ]
    laid = []
    for which in range(sets):
        blocks = []
        for coarse in range(COARSE):
            for out_part in range(2):
                tiles = []
                for half in range(2):
                    for in_part in range(2):
                        tile = (coarse * 2 + (in_part ^ out_part)) * LANES
                        total = jnp.zeros((receivers, LANES), jnp.float32)
                        for k in range(PER_RECV):
                            top = which * count + k * receivers
                            total = jnp.where(
                                seen[k][half],
                                total + wide[top : top + receivers, tile : tile + LANES],
                                total,
                            )
                        tiles.append(-total if in_part == 1 and out_part == 0 else total)
                blocks.append(jnp.concatenate(tiles, axis=1))
        laid.append(jnp.concatenate(blocks, axis=0).astype(jnp.bfloat16))
    return laid


def lay_gains_kernel(tap_ref, slot_rows_ref, out_ref):
    receivers = slot_rows_ref.shape[0] // PER_RECV
    high, low = lay_taps(tap_ref[...], slot_rows_ref[...], receivers, 2)
    rows = high.shape[0]
    out_ref[0:rows, :] = high
    out_ref[rows:, :] = low


def lay_gains(taps, slot_rows):
    vmem = pl.BlockSpec(memory_space=pltpu.VMEM)
    receivers = slot_rows.shape[0] // PER_RECV
    return pl.pallas_call(
        lay_gains_kernel,
        out_shape=jax.ShapeDtypeStruct((4 * COARSE * receivers, 32 * FINE), jnp.bfloat16),
        in_specs=[vmem, vmem],
        out_specs=vmem,
        compiler_params=pltpu.CompilerParams(vmem_limit_bytes=16 * 2**20),
        cost_estimate=pl.CostEstimate(flops=10**9, bytes_accessed=10**6, transcendentals=0),
        name="lay_gains",
    )(taps, slot_rows)


def coarse_sum(spread):
    rows = spread.shape[0] // COARSE
    total = spread[:rows, LANES:]
    for coarse in range(1, COARSE):
        total = total + pltpu.roll(spread[coarse * rows : (coarse + 1) * rows], coarse * FINE, 1)[:, LANES:]
    return total


def moved_ahead(ahead, span):
    moved = [ahead[:, :span].astype(jnp.bfloat16)]
    for coarse in range(1, COARSE):
        moved.append(
            pltpu.roll(ahead, span + LANES - coarse * FINE, 1)[:, :span].astype(jnp.bfloat16)
        )
    return jnp.concatenate(moved, axis=0)


def by_lag(read, rows, store):
    lane = iota((1, LANES), 1)
    for block in range(2):

        def one_slot(j, _, block=block):
            total = jnp.zeros((rows, LANES), jnp.float32)
            for coarse in range(COARSE):
                real = read(coarse, 0, 2 * block) + read(coarse, 1, 2 * block + 1)
                imag = read(coarse, 1, 2 * block) - read(coarse, 0, 2 * block + 1)
                place = coarse * FINE + LANES - j * FINE
                real = pltpu.roll(real, place, 1)
                imag = pltpu.roll(imag, place + DELAYS, 1)
                total = jnp.where(lane >> 4 == coarse, real, total)
                total = jnp.where(lane >> 4 == COARSE + coarse, imag, total)
            store(block * 8 + j, total * (1.0 / 262144.0))
            return 0

        lax.fori_loop(0, 8, one_slot, 0)


def fetch_all(kept_ref, shifted, sems, step_size):
    width = kept_ref.shape[1]
    lead = width % step_size
    steps = width // step_size
    if lead:
        copy_of(kept_ref, shifted, sems, steps, 0, lead).start()
    for step in range(steps):
        copy_of(kept_ref, shifted, sems, step, lead + step * step_size, step_size).start()
    if lead:
        copy_of(kept_ref, shifted, sems, steps, 0, lead).wait()

    def arrive(step):
        copy_of(kept_ref, shifted, sems, step, lead + step * step_size, step_size).wait()

    return arrive


def receive_kernel(
    slot_ref, taps_ref, window_ref, halo_ref, echo_ref,
    received_ref, parts_ref, kept_ref,
    refs_ref, shifted, signal, outer, flipped, tidy, picked, corr, sems,
):
    receivers = echo_ref.shape[0] // 2
    length = echo_ref.shape[1]
    width = length + LANES
    heard_rows = 2 * receivers
    rows = heard_rows + 32
    groups = COARSE * heard_rows
    refs_ref[:, 0:LANES] = halo_ref[...]
    refs_ref[:, LANES:width] = window_ref[...]
    build_shifted(refs_ref, shifted, kept_ref, sems)
    signal[:, 0:LANES] = jnp.zeros((rows, LANES), jnp.bfloat16)
    signal[heard_rows:rows, LANES:width] = refs_ref[:, LANES:width]
    signal[:, width : width + LANES] = jnp.zeros((rows, LANES), jnp.bfloat16)

    def direct(step, _):
        start = pl.multiple_of(step * PIECE, LANES)
        window = shifted[:, pl.ds(start, LANES + PIECE)]
        spread = jnp.dot(
            taps_ref[0:groups, :], window, preferred_element_type=jnp.float32
        ) + jnp.dot(taps_ref[groups:, :], window, preferred_element_type=jnp.float32)
        echo = echo_ref[:, pl.ds(start, PIECE)].astype(jnp.float32)
        heard = (echo + coarse_sum(spread)).astype(jnp.bfloat16)
        received_ref[:, pl.ds(start, PIECE)] = heard
        signal[0:heard_rows, pl.ds(pl.multiple_of(start + LANES, LANES), PIECE)] = heard
        return 0

    lax.fori_loop(0, length // PIECE, direct, 0)
    outer[...] = jnp.zeros(outer.shape, jnp.float32)

    def correlate(step, _):
        start = pl.multiple_of(step * SPAN, LANES)
        outer[...] += lax.dot_general(
            shifted[:, pl.ds(start, SPAN)],
            moved_ahead(signal[:, pl.ds(start, SPAN + LANES)].astype(jnp.float32), SPAN),
            (((1,), (1,)), ((), ())),
            preferred_element_type=jnp.float32,
        )
        return 0

    lax.fori_loop(0, width // SPAN, correlate, 0)
    flipped[...] = jnp.transpose(outer[...])

    def read(coarse, out_part, tile):
        cols = slice(tile * LANES, (tile + 1) * LANES)
        top = coarse * rows + receivers * out_part
        low = coarse * rows + heard_rows + 8 * out_part
        return jnp.concatenate(
            [
                flipped[top : top + receivers, cols],
                flipped[low : low + 8, cols],
                flipped[low + 16 : low + 24, cols],
            ],
            axis=0,
        )

    def store(slot, lags):
        tidy[pl.ds(pl.multiple_of(slot * receivers, receivers), receivers), :] = lags[:receivers]
        corr[pl.ds(pl.multiple_of(slot * 16, 16), 16), :] = lags[receivers:]

    by_lag(read, receivers + 16, store)

    def pick(row, _):
        for k in range(PER_RECV):
            chosen = slot_ref[row, k] * receivers + row
            picked[pl.ds(k * receivers + row, 1), :] = tidy[pl.ds(chosen, 1), :]
        return 0

    lax.fori_loop(0, receivers, pick, 0, unroll=4)
    low = iota((1, LANES), 1) < DELAYS
    for pair in range(PER_RECV // 2):
        even = picked[2 * pair * receivers : (2 * pair + 1) * receivers, :]
        odd = picked[(2 * pair + 1) * receivers : (2 * pair + 2) * receivers, :]
        parts_ref[:, pair * LANES : (pair + 1) * LANES] = jnp.where(
            low, even, pltpu.roll(odd, DELAYS, 1)
        )
        pair += PER_RECV // 2
        parts_ref[:, pair * LANES : (pair + 1) * LANES] = jnp.where(
            low, pltpu.roll(even, DELAYS, 1), odd
        )
    each = 256 // receivers
    for row in range(each):
        tile = PER_RECV + row
        parts_ref[:, tile * LANES : (tile + 1) * LANES] = corr[pl.ds(row, receivers, stride=each), :]

    def sent(step, _):
        copy_of(shifted, kept_ref, sems, step, step * SPAN, SPAN).wait()
        return 0

    lax.fori_loop(0, width // SPAN, sent, 0)


def receive(slot, taps, refs, halo, echoes):
    rows, length = echoes.shape
    receivers = rows // 2
    width = length + LANES
    smem = pl.BlockSpec(memory_space=pltpu.SMEM)
    vmem = pl.BlockSpec(memory_space=pltpu.VMEM)
    products = COARSE * (rows + 32)
    return pl.pallas_call(
        receive_kernel,
        out_shape=(
            jax.ShapeDtypeStruct((rows, length), jnp.bfloat16),
            jax.ShapeDtypeStruct((receivers, PARTS), jnp.float32),
            jax.ShapeDtypeStruct((32 * FINE, width), jnp.bfloat16),
        ),
        in_specs=[smem, vmem, vmem, vmem, vmem],
        out_specs=(vmem, vmem, pl.BlockSpec(memory_space=pl.ANY)),
        scratch_shapes=[
            pltpu.VMEM((32, width), jnp.bfloat16),
            pltpu.VMEM((32 * FINE, width), jnp.bfloat16),
            pltpu.VMEM((rows + 32, width + LANES), jnp.bfloat16),
            pltpu.VMEM((32 * FINE, products), jnp.float32),
            pltpu.VMEM((products, 32 * FINE), jnp.float32),
            pltpu.VMEM((16 * receivers, LANES), jnp.float32),
            pltpu.VMEM((PER_RECV * receivers, LANES), jnp.float32),
            pltpu.VMEM((256, LANES), jnp.float32),
            pltpu.SemaphoreType.DMA((width // SPAN,)),
        ],
        compiler_params=pltpu.CompilerParams(vmem_limit_bytes=52 * 2**20),
        name="receive",
    )(slot, taps, refs, halo, echoes)


def cancel_kernel(
    solved_ref, slot_rows_ref, kept_ref, received_ref, out_ref, weights_ref, taps, shifted, sems
):
    receivers = received_ref.shape[0] // 2
    length = received_ref.shape[1]
    arrive = fetch_all(kept_ref, shifted, sems, PIECE)
    whole = PER_RECV * DELAYS
    weights_ref[0] = solved_ref[:, :whole]
    weights_ref[1] = solved_ref[:, whole:]
    low = iota((1, LANES), 1) < DELAYS
    rows = []
    for pair in range(PER_RECV // 2):
        real = solved_ref[:, pair * LANES : (pair + 1) * LANES]
        imag = solved_ref[:, whole + pair * LANES : whole + (pair + 1) * LANES]
        rows.append(jnp.where(low, real, pltpu.roll(imag, DELAYS, 1)))
        rows.append(jnp.where(low, pltpu.roll(real, DELAYS, 1), imag))
    tap_rows = jnp.concatenate(rows, axis=0).astype(jnp.bfloat16)
    taps[...] = lay_taps(tap_rows, slot_rows_ref[...], receivers, 1)[0]
    piece = PIECE

    def project(step, _):
        start = pl.multiple_of(step * piece, LANES)
        arrive(step)
        spread = jnp.dot(
            taps[...], shifted[:, pl.ds(start, LANES + piece)], preferred_element_type=jnp.float32
        )
        received = received_ref[:, pl.ds(start, piece)].astype(jnp.float32)
        out_ref[:, pl.ds(start, piece)] = (received - coarse_sum(spread)).astype(jnp.bfloat16)
        return 0

    lax.fori_loop(0, length // piece, project, 0)


def cancel(solved, slot_rows, shifted, received):
    rows, length = received.shape
    whole = PER_RECV * DELAYS
    vmem = pl.BlockSpec(memory_space=pltpu.VMEM)
    return pl.pallas_call(
        cancel_kernel,
        out_shape=(
            jax.ShapeDtypeStruct((rows, length), jnp.bfloat16),
            jax.ShapeDtypeStruct((2, rows // 2, whole), jnp.float32),
        ),
        in_specs=[vmem, vmem, pl.BlockSpec(memory_space=pl.ANY), vmem],
        out_specs=(vmem, vmem),
        scratch_shapes=[
            pltpu.VMEM((COARSE * rows, 32 * FINE), jnp.bfloat16),
            pltpu.VMEM((32 * FINE, length + LANES), jnp.bfloat16),
            pltpu.SemaphoreType.DMA((length // PIECE + 1,)),
        ],
        compiler_params=pltpu.CompilerParams(vmem_limit_bytes=RECEIVE_VMEM),
        name="cancel",
    )(solved, slot_rows, shifted, received)


def times_i(packed):
    sign = jnp.where(iota((1, LANES), 1) < DELAYS, -1.0, 1.0)
    count = packed.shape[1] // LANES
    blocks = [
        pltpu.roll(packed[:, b * LANES : (b + 1) * LANES], DELAYS, 1) * sign for b in range(count)
    ]
    return blocks[0] if count == 1 else jnp.concatenate(blocks, axis=1)


def inverse(block):
    size = block.shape[0]
    lane = iota((1, LANES), 1)
    low = lane & (DELAYS - 1)
    sub = iota((size, 1), 0)
    sign = jnp.where(lane < DELAYS, -1.0, 1.0)

    def spread(column):
        return jnp.broadcast_to(block[:, column : column + 1], (size, LANES))

    for first in range(0, size, PANEL):
        col_re = [spread(first + t) for t in range(PANEL)]
        col_im = [spread(DELAYS + first + t) for t in range(PANEL)]
        rows = [block[first + t : first + t + 1, :] for t in range(PANEL)]
        turned_rows = [pltpu.roll(row, DELAYS, 1) * sign for row in rows]
        block = jnp.where((low >= first) & (low < first + PANEL), 0.0, block)
        for t in range(PANEL):
            p = first + t
            over = 1.0 / col_re[t][p : p + 1, :]
            row = jnp.where(lane == p, 1.0, jnp.where(lane == DELAYS + p, 0.0, rows[t])) * over
            turned = (
                jnp.where(lane == DELAYS + p, 1.0, jnp.where(lane == p, 0.0, turned_rows[t])) * over
            )
            for u in range(t + 1, PANEL):
                q = first + u
                below_re = col_re[t][q : q + 1, :]
                below_im = col_im[t][q : q + 1, :]
                fac_re = below_re * over
                fac_im = -below_im * over
                next_re = col_re[u] - col_re[t] * fac_re + col_im[t] * fac_im
                next_im = col_im[u] - col_re[t] * fac_im - col_im[t] * fac_re
                col_re[u] = jnp.where(sub == p, fac_re, next_re)
                col_im[u] = jnp.where(sub == p, fac_im, next_im)
                rows[u] = jnp.where(low == p, 0.0, rows[u]) - below_re * row - below_im * turned
                turned_rows[u] = (
                    jnp.where(low == p, 0.0, turned_rows[u]) - below_re * turned + below_im * row
                )
            later = (low > p) & (low < first + PANEL)
            row = jnp.where(later, 0.0, row)
            turned = jnp.where(later, 0.0, turned)
            block = block - col_re[t] * row - col_im[t] * turned
            block = jnp.where(sub == p, row, block)
    return block


def exact_dot(left, right):
    return jnp.dot(left, right, precision=HIGHEST, preferred_element_type=jnp.float32)


def three_parts(array):
    high = array.astype(jnp.bfloat16)
    rest = array - high.astype(jnp.float32)
    middle = rest.astype(jnp.bfloat16)
    return high, middle, (rest - middle.astype(jnp.float32)).astype(jnp.bfloat16)


def deep_dot(left, right):
    lh, lm, ll = three_parts(left)
    rh, rm, rl = three_parts(right)
    return jnp.dot(
        jnp.concatenate([ll, lh, lm, lm, lh, lh], axis=1),
        jnp.concatenate([rh, rl, rm, rh, rm, rh], axis=0),
        preferred_element_type=jnp.float32,
    )


def solve_kernel(slot_ref, corr_ref, cross_ref, out_ref, system, pairs):
    count = PER_RECV
    size = DELAYS
    for k in range(count):
        for l in range(count):
            row = k * count + l
            ahead = slot_ref[k] * 16 + slot_ref[l]
            behind = slot_ref[l] * 16 + slot_ref[k]
            pairs[row : row + 1, 0:LANES] = corr_ref[pl.ds(ahead, 1), :]
            pairs[row : row + 1, LANES : 2 * LANES] = corr_ref[pl.ds(behind, 1), :]
    pairs[count * count :, :] = jnp.zeros((pairs.shape[0] - count * count, 2 * LANES), jnp.float32)
    src = iota((2 * LANES, 2 * LANES), 0)
    dst = iota((2 * LANES, 2 * LANES), 1)
    x = dst & (LANES - 1)
    imag = dst >> 7
    from_ahead = jnp.where(x > size, imag * size + LANES - x, jnp.where(x == 0, imag * size, -1))
    from_behind_lag = jnp.where((x > 0) & (x < size), LANES + imag * size + x, -1)
    order = jnp.where(src == from_ahead, 1.0, 0.0) + jnp.where(
        src == from_behind_lag, jnp.where(imag == 1, -1.0, 1.0), 0.0
    )
    circular = exact_dot(pairs[...], order)
    lane = iota((1, LANES), 1)
    sub = iota((size, 1), 0)
    for k in range(count):
        for l in range(count):
            row = k * count + l
            real = jnp.broadcast_to(circular[row : row + 1, 0:LANES], (size, LANES))
            imag_part = jnp.broadcast_to(circular[row : row + 1, LANES:], (size, LANES))
            real = pltpu.roll(real, 0, 1, stride=1, stride_axis=0)
            imag_part = pltpu.roll(imag_part, size, 1, stride=1, stride_axis=0)
            block = jnp.where(lane < size, real, imag_part)
            if k == l:
                block = block + jnp.where(lane == sub, loading, 0.0)
            system[k * size : (k + 1) * size, l * LANES : (l + 1) * LANES] = block
    unit = jnp.where(lane == sub, 1.0, 0.0)

    def eliminate(i, _):
        mine = pl.ds(pl.multiple_of(i * size, size), size)
        col = pl.ds(pl.multiple_of(i * LANES, LANES), LANES)
        over = inverse(system[mine, col])
        system[mine, col] = unit
        right = system[mine, :]
        scaled = deep_dot(over, jnp.concatenate([right, times_i(right)], axis=0))
        factors = system[:, col]
        system[:, col] = jnp.zeros((count * size, LANES), jnp.float32)
        both = jnp.concatenate([scaled, times_i(scaled)], axis=0)
        system[...] = system[...] - deep_dot(factors, both)
        system[mine, :] = scaled
        return 0

    lax.fori_loop(0, count, eliminate, 0)
    whole = count * size
    total = cross_ref[...]
    sides = jnp.concatenate(
        [total[:, :whole], total[:, whole:], jnp.zeros((6, whole), jnp.float32)], axis=0
    )
    found = exact_dot(sides, system[...])
    rows = []
    for k in range(count):
        by_real = found[0:1, k * LANES : (k + 1) * LANES]
        by_imag = found[1:2, k * LANES : (k + 1) * LANES]
        rows.append(jnp.where(lane < size, by_real, -by_real) + pltpu.roll(by_imag, size, 1))
    for pair in range(count // 2):
        even, odd = rows[2 * pair], rows[2 * pair + 1]
        real = jnp.where(lane < size, even, pltpu.roll(odd, size, 1))
        imag = jnp.where(lane < size, pltpu.roll(even, size, 1), odd)
        low, high = pair * LANES, whole + pair * LANES
        shape = (out_ref.shape[0], LANES)
        out_ref[:, low : low + LANES] = jnp.broadcast_to(real, shape)
        out_ref[:, high : high + LANES] = jnp.broadcast_to(imag, shape)


def solve(slot, corr, cross, peers):
    smem = pl.BlockSpec(memory_space=pltpu.SMEM)
    vmem = pl.BlockSpec(memory_space=pltpu.VMEM)
    size = PER_RECV * DELAYS
    return pl.pallas_call(
        solve_kernel,
        out_shape=jax.ShapeDtypeStruct((peers, PER_RECV * LANES), jnp.float32),
        in_specs=[smem, vmem, vmem],
        out_specs=vmem,
        scratch_shapes=[
            pltpu.VMEM((size, PER_RECV * LANES), jnp.float32),
            pltpu.VMEM((40, 2 * LANES), jnp.float32),
        ],
        compiler_params=pltpu.CompilerParams(vmem_limit_bytes=16 * 2**20),
        name="solve",
    )(slot, corr, cross)


def local(symbols, incidence, delays, gains, echoes):
    owned, length = symbols.shape
    chan_count = lax.axis_size("chan")
    chan_index = lax.axis_index("chan")
    tm_count = lax.axis_size("tm")
    tm_index = lax.axis_index("tm")
    recv_count = echoes.shape[1]
    sent = symbols.astype(jnp.bfloat16)
    next_symbols = passed_along(sent, "chan", -1)
    refs = remodulate(sent, next_symbols)
    halo = from_behind(refs[:, length - LANES :], "tm", 1)
    owner_chan = incidence // owned
    slot = (owner_chan - chan_index) % chan_count * owned + incidence % owned
    slot_rows = jnp.broadcast_to(
        slot.T.reshape(PER_RECV * recv_count, 1), (PER_RECV * recv_count, LANES)
    )
    lag = jnp.arange(LANES, dtype=jnp.int32)
    gain_rows = jnp.where(
        lag < DELAYS,
        gains[0].T.reshape(PER_RECV * recv_count, 1),
        gains[1].T.reshape(PER_RECV * recv_count, 1),
    )
    gain_taps = jnp.where(
        delays.T.reshape(PER_RECV * recv_count, 1) == (lag & (DELAYS - 1)), gain_rows, 0.0
    )
    tap_high = lax.reduce_precision(gain_taps, 8, 7)
    tap_low = (gain_taps - tap_high).astype(jnp.bfloat16)
    gain_rows = jnp.concatenate([tap_high.astype(jnp.bfloat16), tap_low], axis=0)
    laid = lay_gains(gain_rows, slot_rows)
    received, parts, shifted = receive(
        slot, laid, refs, halo, echoes.reshape(2 * recv_count, length)
    )
    share = recv_count // tm_count
    corr_share = 256 * LANES // tm_count
    parts = jnp.sum(lax.all_to_all(parts, "tm", 0, 0, tiled=True), axis=0, keepdims=True)
    my_cross = parts[:, : PER_RECV * LANES]
    my_corr = jnp.broadcast_to(parts[:, PER_RECV * LANES :], (tm_count, corr_share))
    corr = lax.all_to_all(my_corr, "tm", 0, 0, tiled=True).reshape(256, LANES)
    my_slot = lax.dynamic_slice_in_dim(slot, tm_index * share, share, 0).reshape(PER_RECV)
    mine = solve(my_slot, corr, my_cross, tm_count)
    solved = lax.all_to_all(mine, "tm", 0, 0, tiled=True)
    cancelled, weights = cancel(solved, slot_rows, shifted, received)
    return (cancelled.reshape(2, recv_count, length), weights)


def solution(mesh):
    in_specs = (
        P("chan", "tm"),
        P("chan", None),
        P("chan", None),
        P(None, "chan", None),
        P(None, "chan", "tm"),
    )
    out_specs = (P(None, "chan", "tm"), P(None, "chan", None))
    return jax.shard_map(local, mesh=mesh, in_specs=in_specs, out_specs=out_specs, check_vma=False)
```

```python
import math

import jax
import jax.numpy as jnp
import numpy as np
from jax import lax
from jax.experimental import pallas as pl
from jax.experimental.pallas import tpu as pltpu
from jax.sharding import PartitionSpec as P

ACTIVE = 6817
DELAYS = 64
PER_RECV = 6
LANES = 128
FINE = 16
COARSE = DELAYS // FINE
PARTS = PER_RECV * LANES + 1024
PANEL = 4
SPAN = 1664
PIECE = 4096
RECEIVE_VMEM = 56 * 2**20


loading = 0.1
HIGHEST = lax.Precision.HIGHEST


def passed_along(array, axis, by):
    peers = lax.axis_size(axis)
    return lax.ppermute(array, axis, [(i, (i + by) % peers) for i in range(peers)])


def from_behind(block, axis, distance):
    devices = range(lax.axis_size(axis))
    route = [(i - distance, i) for i in devices if i - distance in devices]
    return lax.ppermute(block, axis, route)


def parts_of(table, count):
    parts = []
    for _ in range(count):
        part = table.astype(jnp.bfloat16).astype(np.float64)
        parts.append(part)
        table = table - part
    return parts


def wave_tables(length):
    tiles = length // LANES
    turn = 2.0 * np.pi / tiles

    def real_form(angle):
        return np.block([[np.cos(angle), -np.sin(angle)], [np.sin(angle), np.cos(angle)]])

    q = np.arange(tiles)
    v = np.arange(LANES)
    first = real_form(turn * ((q[:, None] * q[None, :]) % tiles))
    second = real_form(turn * ((q[:, None] * v[None, :]) % tiles))
    angle = 2.0 * np.pi / length * (v[:, None] * v[None, :])
    size = (1 - 2 * (v % 2))[:, None] / math.sqrt(ACTIVE * 42.0)
    high, low = parts_of(second, 2)
    return np.concatenate(
        [*parts_of(first, 3), low, high, high, np.cos(angle) * size, np.sin(angle) * size],
        axis=1,
        dtype=np.float32,
    )


def remodulate_kernel(own_ref, next_ref, table_ref, out_ref, points, samples):
    owned, length = own_ref.shape
    emitters = 2 * owned
    first = table_ref[:, 0 : 3 * LANES].astype(jnp.bfloat16)
    second = table_ref[:, 3 * LANES : 9 * LANES].astype(jnp.bfloat16)
    along = table_ref[:, 9 * LANES : 10 * LANES]
    across = table_ref[:, 10 * LANES :]
    tiles = length // LANES
    for q in range(tiles):
        cols = slice(q * LANES, (q + 1) * LANES)
        symbol = jnp.concatenate([own_ref[:, cols], next_ref[:, cols]], axis=0).astype(jnp.float32)
        column = jnp.floor(symbol * 0.125)
        tone = iota((1, LANES), 1) + (q * LANES - length // 2)
        used = (tone <= (ACTIVE - 1) // 2) & (tone >= -((ACTIVE - 1) // 2))
        rows = slice(q * emitters, (q + 1) * emitters)
        points[0, rows, :] = jnp.where(used, 2.0 * (symbol - 8.0 * column) - 7.0, 0.0)
        points[1, rows, :] = jnp.where(used, 2.0 * column - 7.0, 0.0)
    every = [pl.ds(n, tiles, stride=emitters) for n in range(emitters)]
    grid = jnp.concatenate(
        [
            jnp.concatenate([points[part, rows, :] for rows in every], axis=1).astype(jnp.bfloat16)
            for part in range(2)
        ],
        axis=0,
    )
    partial = jnp.dot(
        first, jnp.concatenate([grid] * 3, axis=0), preferred_element_type=jnp.float32
    )
    turned = []
    for n in range(emitters):
        cols = slice(n * LANES, (n + 1) * LANES)
        real = jnp.concatenate([partial[:tiles, cols]] * 2, axis=0)
        imag = jnp.concatenate([partial[tiles:, cols]] * 2, axis=0)
        turned.append(
            jnp.concatenate(
                [
                    real * along - imag * across,
                    real * across + imag * along,
                ],
                axis=1,
            )
        )
    turned = jnp.concatenate(turned, axis=0)
    high = turned.astype(jnp.bfloat16)
    low = (turned - high.astype(jnp.float32)).astype(jnp.bfloat16)
    wave = lax.dot_general(
        second,
        jnp.concatenate([high, low, high], axis=1),
        (((1,), (1,)), ((), ())),
        preferred_element_type=jnp.float32,
    )
    for part in range(2):
        for n in range(emitters):
            samples[part, every[n], :] = wave[
                part * tiles : (part + 1) * tiles, n * LANES : (n + 1) * LANES
            ]
    for q in range(tiles):
        out_ref[:, q * LANES : (q + 1) * LANES] = jnp.concatenate(
            [
                samples[part, q * emitters + side * owned : q * emitters + (side + 1) * owned, :]
                for side in range(2)
                for part in range(2)
            ],
            axis=0,
        ).astype(jnp.bfloat16)


def remodulate(own, following):
    owned, length = own.shape
    emitters = 2 * owned
    vmem = pl.BlockSpec(memory_space=pltpu.VMEM)
    return pl.pallas_call(
        remodulate_kernel,
        out_shape=jax.ShapeDtypeStruct((2 * emitters, length), jnp.bfloat16),
        in_specs=[vmem] * 3,
        out_specs=vmem,
        scratch_shapes=[
            pltpu.VMEM((2, emitters * length // LANES, LANES), jnp.float32),
            pltpu.VMEM((2, emitters * length // LANES, LANES), jnp.float32),
        ],
        compiler_params=pltpu.CompilerParams(vmem_limit_bytes=24 * 2**20),
        cost_estimate=pl.CostEstimate(flops=2 * 10**9, bytes_accessed=10**6, transcendentals=0),
        name="remodulate",
    )(own, following, jnp.asarray(wave_tables(length)))


def iota(shape, axis):
    return lax.broadcasted_iota(jnp.int32, shape, axis)


def copy_of(source, target, sems, step, start, size):
    cols = pl.ds(pl.multiple_of(start, LANES), size)
    return pltpu.make_async_copy(source.at[:, cols], target.at[:, cols], sems.at[step])


def build_shifted(ref_ref, shifted_ref, kept_ref, sems):
    rows, width = ref_ref.shape
    piece = SPAN

    def one_piece(step, _):
        start = pl.multiple_of(step * piece, LANES)
        before = pl.multiple_of(jnp.maximum(start - LANES, 0), LANES)
        first = ref_ref[:, pl.ds(before, LANES)].astype(jnp.float32)
        body = ref_ref[:, pl.ds(start, piece)].astype(jnp.float32)
        source = jnp.concatenate([first, body], axis=1)
        for row in range(rows):
            spread = jnp.broadcast_to(source[row : row + 1, :], (FINE, LANES + piece))
            rolled = pltpu.roll(spread, 0, 1, stride=1, stride_axis=0)
            shifted_ref[row * FINE : (row + 1) * FINE, pl.ds(start, piece)] = rolled[
                :, LANES:
            ].astype(jnp.bfloat16)
        copy_of(shifted_ref, kept_ref, sems, step, start, piece).start()
        return 0

    lax.fori_loop(0, width // piece, one_piece, 0)


def lay_taps(tap_rows, slot_rows, receivers, sets):
    lane = iota((LANES, LANES), 1)
    source = iota((LANES, LANES), 0)
    spread = jnp.concatenate(
        [
            jnp.where(source == part * DELAYS + coarse * FINE + (lane & (FINE - 1)), 1.0, 0.0)
            for coarse in range(COARSE)
            for part in range(2)
        ],
        axis=1,
    )
    wide = jnp.dot(tap_rows, spread.astype(jnp.bfloat16), preferred_element_type=jnp.float32)
    here = iota((1, LANES), 1) >> 4
    count = PER_RECV * receivers
    seen = [
        [slot_rows[k * receivers : (k + 1) * receivers, :] == half * 8 + here for half in range(2)]
        for k in range(PER_RECV)
    ]
    laid = []
    for which in range(sets):
        blocks = []
        for coarse in range(COARSE):
            for out_part in range(2):
                tiles = []
                for half in range(2):
                    for in_part in range(2):
                        tile = (coarse * 2 + (in_part ^ out_part)) * LANES
                        total = jnp.zeros((receivers, LANES), jnp.float32)
                        for k in range(PER_RECV):
                            top = which * count + k * receivers
                            total = jnp.where(
                                seen[k][half],
                                total + wide[top : top + receivers, tile : tile + LANES],
                                total,
                            )
                        tiles.append(-total if in_part == 1 and out_part == 0 else total)
                blocks.append(jnp.concatenate(tiles, axis=1))
        laid.append(jnp.concatenate(blocks, axis=0).astype(jnp.bfloat16))
    return laid


def lay_gains_kernel(tap_ref, slot_rows_ref, out_ref):
    receivers = slot_rows_ref.shape[0] // PER_RECV
    high, low = lay_taps(tap_ref[...], slot_rows_ref[...], receivers, 2)
    rows = high.shape[0]
    out_ref[0:rows, :] = high
    out_ref[rows:, :] = low


def lay_gains(taps, slot_rows):
    vmem = pl.BlockSpec(memory_space=pltpu.VMEM)
    receivers = slot_rows.shape[0] // PER_RECV
    return pl.pallas_call(
        lay_gains_kernel,
        out_shape=jax.ShapeDtypeStruct((4 * COARSE * receivers, 32 * FINE), jnp.bfloat16),
        in_specs=[vmem, vmem],
        out_specs=vmem,
        compiler_params=pltpu.CompilerParams(vmem_limit_bytes=16 * 2**20),
        cost_estimate=pl.CostEstimate(flops=10**9, bytes_accessed=10**6, transcendentals=0),
        name="lay_gains",
    )(taps, slot_rows)


def coarse_sum(spread):
    rows = spread.shape[0] // COARSE
    total = spread[:rows, LANES:]
    for coarse in range(1, COARSE):
        total = total + pltpu.roll(spread[coarse * rows : (coarse + 1) * rows], coarse * FINE, 1)[:, LANES:]
    return total


def moved_ahead(ahead, span):
    moved = [ahead[:, :span].astype(jnp.bfloat16)]
    for coarse in range(1, COARSE):
        moved.append(
            pltpu.roll(ahead, span + LANES - coarse * FINE, 1)[:, :span].astype(jnp.bfloat16)
        )
    return jnp.concatenate(moved, axis=0)


def by_lag(read, rows, store):
    lane = iota((1, LANES), 1)
    for block in range(2):

        def one_slot(j, _, block=block):
            total = jnp.zeros((rows, LANES), jnp.float32)
            for coarse in range(COARSE):
                real = read(coarse, 0, 2 * block) + read(coarse, 1, 2 * block + 1)
                imag = read(coarse, 1, 2 * block) - read(coarse, 0, 2 * block + 1)
                place = coarse * FINE + LANES - j * FINE
                real = pltpu.roll(real, place, 1)
                imag = pltpu.roll(imag, place + DELAYS, 1)
                total = jnp.where(lane >> 4 == coarse, real, total)
                total = jnp.where(lane >> 4 == COARSE + coarse, imag, total)
            store(block * 8 + j, total * (1.0 / 262144.0))
            return 0

        lax.fori_loop(0, 8, one_slot, 0)


def fetch_all(kept_ref, shifted, sems, step_size):
    width = kept_ref.shape[1]
    lead = width % step_size
    steps = width // step_size
    if lead:
        copy_of(kept_ref, shifted, sems, steps, 0, lead).start()
    for step in range(steps):
        copy_of(kept_ref, shifted, sems, step, lead + step * step_size, step_size).start()
    if lead:
        copy_of(kept_ref, shifted, sems, steps, 0, lead).wait()

    def arrive(step):
        copy_of(kept_ref, shifted, sems, step, lead + step * step_size, step_size).wait()

    return arrive


def receive_kernel(
    slot_ref, taps_ref, window_ref, halo_ref, echo_ref,
    received_ref, parts_ref, kept_ref,
    refs_ref, shifted, signal, outer, flipped, tidy, picked, corr, sems,
):
    receivers = echo_ref.shape[0] // 2
    length = echo_ref.shape[1]
    width = length + LANES
    heard_rows = 2 * receivers
    rows = heard_rows + 32
    groups = COARSE * heard_rows
    refs_ref[:, 0:LANES] = halo_ref[...]
    refs_ref[:, LANES:width] = window_ref[...]
    build_shifted(refs_ref, shifted, kept_ref, sems)
    signal[:, 0:LANES] = jnp.zeros((rows, LANES), jnp.bfloat16)
    signal[heard_rows:rows, LANES:width] = refs_ref[:, LANES:width]
    signal[:, width : width + LANES] = jnp.zeros((rows, LANES), jnp.bfloat16)

    def direct(step, _):
        start = pl.multiple_of(step * PIECE, LANES)
        window = shifted[:, pl.ds(start, LANES + PIECE)]
        spread = jnp.dot(
            taps_ref[0:groups, :], window, preferred_element_type=jnp.float32
        ) + jnp.dot(taps_ref[groups:, :], window, preferred_element_type=jnp.float32)
        echo = echo_ref[:, pl.ds(start, PIECE)].astype(jnp.float32)
        heard = (echo + coarse_sum(spread)).astype(jnp.bfloat16)
        received_ref[:, pl.ds(start, PIECE)] = heard
        signal[0:heard_rows, pl.ds(pl.multiple_of(start + LANES, LANES), PIECE)] = heard
        return 0

    lax.fori_loop(0, length // PIECE, direct, 0)
    outer[...] = jnp.zeros(outer.shape, jnp.float32)

    def correlate(step, _):
        start = pl.multiple_of(step * SPAN, LANES)
        outer[...] += lax.dot_general(
            shifted[:, pl.ds(start, SPAN)],
            moved_ahead(signal[:, pl.ds(start, SPAN + LANES)].astype(jnp.float32), SPAN),
            (((1,), (1,)), ((), ())),
            preferred_element_type=jnp.float32,
        )
        return 0

    lax.fori_loop(0, width // SPAN, correlate, 0)
    flipped[...] = jnp.transpose(outer[...])

    def read(coarse, out_part, tile):
        cols = slice(tile * LANES, (tile + 1) * LANES)
        top = coarse * rows + receivers * out_part
        low = coarse * rows + heard_rows + 8 * out_part
        return jnp.concatenate(
            [
                flipped[top : top + receivers, cols],
                flipped[low : low + 8, cols],
                flipped[low + 16 : low + 24, cols],
            ],
            axis=0,
        )

    def store(slot, lags):
        tidy[pl.ds(pl.multiple_of(slot * receivers, receivers), receivers), :] = lags[:receivers]
        corr[pl.ds(pl.multiple_of(slot * 16, 16), 16), :] = lags[receivers:]

    by_lag(read, receivers + 16, store)

    def pick(row, _):
        for k in range(PER_RECV):
            chosen = slot_ref[row, k] * receivers + row
            picked[pl.ds(k * receivers + row, 1), :] = tidy[pl.ds(chosen, 1), :]
        return 0

    lax.fori_loop(0, receivers, pick, 0, unroll=4)
    low = iota((1, LANES), 1) < DELAYS
    for pair in range(PER_RECV // 2):
        even = picked[2 * pair * receivers : (2 * pair + 1) * receivers, :]
        odd = picked[(2 * pair + 1) * receivers : (2 * pair + 2) * receivers, :]
        parts_ref[:, pair * LANES : (pair + 1) * LANES] = jnp.where(
            low, even, pltpu.roll(odd, DELAYS, 1)
        )
        pair += PER_RECV // 2
        parts_ref[:, pair * LANES : (pair + 1) * LANES] = jnp.where(
            low, pltpu.roll(even, DELAYS, 1), odd
        )
    each = 256 // receivers
    for row in range(each):
        tile = PER_RECV + row
        parts_ref[:, tile * LANES : (tile + 1) * LANES] = corr[pl.ds(row, receivers, stride=each), :]

    def sent(step, _):
        copy_of(shifted, kept_ref, sems, step, step * SPAN, SPAN).wait()
        return 0

    lax.fori_loop(0, width // SPAN, sent, 0)


def receive(slot, taps, refs, halo, echoes):
    rows, length = echoes.shape
    receivers = rows // 2
    width = length + LANES
    smem = pl.BlockSpec(memory_space=pltpu.SMEM)
    vmem = pl.BlockSpec(memory_space=pltpu.VMEM)
    products = COARSE * (rows + 32)
    return pl.pallas_call(
        receive_kernel,
        out_shape=(
            jax.ShapeDtypeStruct((rows, length), jnp.bfloat16),
            jax.ShapeDtypeStruct((receivers, PARTS), jnp.float32),
            jax.ShapeDtypeStruct((32 * FINE, width), jnp.bfloat16),
        ),
        in_specs=[smem, vmem, vmem, vmem, vmem],
        out_specs=(vmem, vmem, pl.BlockSpec(memory_space=pl.ANY)),
        scratch_shapes=[
            pltpu.VMEM((32, width), jnp.bfloat16),
            pltpu.VMEM((32 * FINE, width), jnp.bfloat16),
            pltpu.VMEM((rows + 32, width + LANES), jnp.bfloat16),
            pltpu.VMEM((32 * FINE, products), jnp.float32),
            pltpu.VMEM((products, 32 * FINE), jnp.float32),
            pltpu.VMEM((16 * receivers, LANES), jnp.float32),
            pltpu.VMEM((PER_RECV * receivers, LANES), jnp.float32),
            pltpu.VMEM((256, LANES), jnp.float32),
            pltpu.SemaphoreType.DMA((width // SPAN,)),
        ],
        compiler_params=pltpu.CompilerParams(vmem_limit_bytes=52 * 2**20),
        name="receive",
    )(slot, taps, refs, halo, echoes)


def cancel_kernel(
    solved_ref, slot_rows_ref, kept_ref, received_ref, out_ref, weights_ref, taps, shifted, sems
):
    receivers = received_ref.shape[0] // 2
    length = received_ref.shape[1]
    arrive = fetch_all(kept_ref, shifted, sems, PIECE)
    whole = PER_RECV * DELAYS
    weights_ref[0] = solved_ref[:, :whole]
    weights_ref[1] = solved_ref[:, whole:]
    low = iota((1, LANES), 1) < DELAYS
    rows = []
    for pair in range(PER_RECV // 2):
        real = solved_ref[:, pair * LANES : (pair + 1) * LANES]
        imag = solved_ref[:, whole + pair * LANES : whole + (pair + 1) * LANES]
        rows.append(jnp.where(low, real, pltpu.roll(imag, DELAYS, 1)))
        rows.append(jnp.where(low, pltpu.roll(real, DELAYS, 1), imag))
    tap_rows = jnp.concatenate(rows, axis=0).astype(jnp.bfloat16)
    taps[...] = lay_taps(tap_rows, slot_rows_ref[...], receivers, 1)[0]
    piece = PIECE

    def project(step, _):
        start = pl.multiple_of(step * piece, LANES)
        arrive(step)
        spread = jnp.dot(
            taps[...], shifted[:, pl.ds(start, LANES + piece)], preferred_element_type=jnp.float32
        )
        received = received_ref[:, pl.ds(start, piece)].astype(jnp.float32)
        out_ref[:, pl.ds(start, piece)] = (received - coarse_sum(spread)).astype(jnp.bfloat16)
        return 0

    lax.fori_loop(0, length // piece, project, 0)


def cancel(solved, slot_rows, shifted, received):
    rows, length = received.shape
    whole = PER_RECV * DELAYS
    vmem = pl.BlockSpec(memory_space=pltpu.VMEM)
    return pl.pallas_call(
        cancel_kernel,
        out_shape=(
            jax.ShapeDtypeStruct((rows, length), jnp.bfloat16),
            jax.ShapeDtypeStruct((2, rows // 2, whole), jnp.float32),
        ),
        in_specs=[vmem, vmem, pl.BlockSpec(memory_space=pl.ANY), vmem],
        out_specs=(vmem, vmem),
        scratch_shapes=[
            pltpu.VMEM((COARSE * rows, 32 * FINE), jnp.bfloat16),
            pltpu.VMEM((32 * FINE, length + LANES), jnp.bfloat16),
            pltpu.SemaphoreType.DMA((length // PIECE + 1,)),
        ],
        compiler_params=pltpu.CompilerParams(vmem_limit_bytes=RECEIVE_VMEM),
        name="cancel",
    )(solved, slot_rows, shifted, received)


def times_i(packed):
    sign = jnp.where(iota((1, LANES), 1) < DELAYS, -1.0, 1.0)
    count = packed.shape[1] // LANES
    blocks = [
        pltpu.roll(packed[:, b * LANES : (b + 1) * LANES], DELAYS, 1) * sign for b in range(count)
    ]
    return blocks[0] if count == 1 else jnp.concatenate(blocks, axis=1)


def inverse(block):
    size = block.shape[0]
    lane = iota((1, LANES), 1)
    low = lane & (DELAYS - 1)
    sub = iota((size, 1), 0)
    sign = jnp.where(lane < DELAYS, -1.0, 1.0)

    def spread(column):
        return jnp.broadcast_to(block[:, column : column + 1], (size, LANES))

    for first in range(0, size, PANEL):
        col_re = [spread(first + t) for t in range(PANEL)]
        col_im = [spread(DELAYS + first + t) for t in range(PANEL)]
        rows = [block[first + t : first + t + 1, :] for t in range(PANEL)]
        turned_rows = [pltpu.roll(row, DELAYS, 1) * sign for row in rows]
        block = jnp.where((low >= first) & (low < first + PANEL), 0.0, block)
        for t in range(PANEL):
            p = first + t
            over = 1.0 / col_re[t][p : p + 1, :]
            row = jnp.where(lane == p, 1.0, jnp.where(lane == DELAYS + p, 0.0, rows[t])) * over
            turned = (
                jnp.where(lane == DELAYS + p, 1.0, jnp.where(lane == p, 0.0, turned_rows[t])) * over
            )
            for u in range(t + 1, PANEL):
                q = first + u
                below_re = col_re[t][q : q + 1, :]
                below_im = col_im[t][q : q + 1, :]
                fac_re = below_re * over
                fac_im = -below_im * over
                next_re = col_re[u] - col_re[t] * fac_re + col_im[t] * fac_im
                next_im = col_im[u] - col_re[t] * fac_im - col_im[t] * fac_re
                col_re[u] = jnp.where(sub == p, fac_re, next_re)
                col_im[u] = jnp.where(sub == p, fac_im, next_im)
                rows[u] = jnp.where(low == p, 0.0, rows[u]) - below_re * row - below_im * turned
                turned_rows[u] = (
                    jnp.where(low == p, 0.0, turned_rows[u]) - below_re * turned + below_im * row
                )
            later = (low > p) & (low < first + PANEL)
            row = jnp.where(later, 0.0, row)
            turned = jnp.where(later, 0.0, turned)
            block = block - col_re[t] * row - col_im[t] * turned
            block = jnp.where(sub == p, row, block)
    return block


def exact_dot(left, right):
    return jnp.dot(left, right, precision=HIGHEST, preferred_element_type=jnp.float32)


def three_parts(array):
    high = array.astype(jnp.bfloat16)
    rest = array - high.astype(jnp.float32)
    middle = rest.astype(jnp.bfloat16)
    return high, middle, (rest - middle.astype(jnp.float32)).astype(jnp.bfloat16)


def deep_dot(left, right):
    lh, lm, ll = three_parts(left)
    rh, rm, rl = three_parts(right)
    return jnp.dot(
        jnp.concatenate([ll, lh, lm, lm, lh, lh], axis=1),
        jnp.concatenate([rh, rl, rm, rh, rm, rh], axis=0),
        preferred_element_type=jnp.float32,
    )


def solve_kernel(slot_ref, corr_ref, cross_ref, out_ref, system, pairs):
    count = PER_RECV
    size = DELAYS
    for k in range(count):
        for l in range(count):
            row = k * count + l
            ahead = slot_ref[k] * 16 + slot_ref[l]
            behind = slot_ref[l] * 16 + slot_ref[k]
            pairs[row : row + 1, 0:LANES] = corr_ref[pl.ds(ahead, 1), :]
            pairs[row : row + 1, LANES : 2 * LANES] = corr_ref[pl.ds(behind, 1), :]
    pairs[count * count :, :] = jnp.zeros((pairs.shape[0] - count * count, 2 * LANES), jnp.float32)
    src = iota((2 * LANES, 2 * LANES), 0)
    dst = iota((2 * LANES, 2 * LANES), 1)
    x = dst & (LANES - 1)
    imag = dst >> 7
    from_ahead = jnp.where(x > size, imag * size + LANES - x, jnp.where(x == 0, imag * size, -1))
    from_behind_lag = jnp.where((x > 0) & (x < size), LANES + imag * size + x, -1)
    order = jnp.where(src == from_ahead, 1.0, 0.0) + jnp.where(
        src == from_behind_lag, jnp.where(imag == 1, -1.0, 1.0), 0.0
    )
    circular = exact_dot(pairs[...], order)
    lane = iota((1, LANES), 1)
    sub = iota((size, 1), 0)
    for k in range(count):
        for l in range(count):
            row = k * count + l
            real = jnp.broadcast_to(circular[row : row + 1, 0:LANES], (size, LANES))
            imag_part = jnp.broadcast_to(circular[row : row + 1, LANES:], (size, LANES))
            real = pltpu.roll(real, 0, 1, stride=1, stride_axis=0)
            imag_part = pltpu.roll(imag_part, size, 1, stride=1, stride_axis=0)
            block = jnp.where(lane < size, real, imag_part)
            if k == l:
                block = block + jnp.where(lane == sub, loading, 0.0)
            system[k * size : (k + 1) * size, l * LANES : (l + 1) * LANES] = block
    unit = jnp.where(lane == sub, 1.0, 0.0)

    def eliminate(i, _):
        mine = pl.ds(pl.multiple_of(i * size, size), size)
        col = pl.ds(pl.multiple_of(i * LANES, LANES), LANES)
        over = inverse(system[mine, col])
        system[mine, col] = unit
        right = system[mine, :]
        scaled = deep_dot(over, jnp.concatenate([right, times_i(right)], axis=0))
        factors = system[:, col]
        system[:, col] = jnp.zeros((count * size, LANES), jnp.float32)
        both = jnp.concatenate([scaled, times_i(scaled)], axis=0)
        system[...] = system[...] - deep_dot(factors, both)
        system[mine, :] = scaled
        return 0

    lax.fori_loop(0, count, eliminate, 0)
    whole = count * size
    total = cross_ref[...]
    sides = jnp.concatenate(
        [total[:, :whole], total[:, whole:], jnp.zeros((6, whole), jnp.float32)], axis=0
    )
    found = exact_dot(sides, system[...])
    rows = []
    for k in range(count):
        by_real = found[0:1, k * LANES : (k + 1) * LANES]
        by_imag = found[1:2, k * LANES : (k + 1) * LANES]
        rows.append(jnp.where(lane < size, by_real, -by_real) + pltpu.roll(by_imag, size, 1))
    for pair in range(count // 2):
        even, odd = rows[2 * pair], rows[2 * pair + 1]
        real = jnp.where(lane < size, even, pltpu.roll(odd, size, 1))
        imag = jnp.where(lane < size, pltpu.roll(even, size, 1), odd)
        low, high = pair * LANES, whole + pair * LANES
        shape = (out_ref.shape[0], LANES)
        out_ref[:, low : low + LANES] = jnp.broadcast_to(real, shape)
        out_ref[:, high : high + LANES] = jnp.broadcast_to(imag, shape)


def solve(slot, corr, cross, peers):
    smem = pl.BlockSpec(memory_space=pltpu.SMEM)
    vmem = pl.BlockSpec(memory_space=pltpu.VMEM)
    size = PER_RECV * DELAYS
    return pl.pallas_call(
        solve_kernel,
        out_shape=jax.ShapeDtypeStruct((peers, PER_RECV * LANES), jnp.float32),
        in_specs=[smem, vmem, vmem],
        out_specs=vmem,
        scratch_shapes=[
            pltpu.VMEM((size, PER_RECV * LANES), jnp.float32),
            pltpu.VMEM((40, 2 * LANES), jnp.float32),
        ],
        compiler_params=pltpu.CompilerParams(vmem_limit_bytes=16 * 2**20),
        name="solve",
    )(slot, corr, cross)


def local(symbols, incidence, delays, gains, echoes):
    owned, length = symbols.shape
    chan_count = lax.axis_size("chan")
    chan_index = lax.axis_index("chan")
    tm_count = lax.axis_size("tm")
    tm_index = lax.axis_index("tm")
    recv_count = echoes.shape[1]
    sent = symbols.astype(jnp.bfloat16)
    next_symbols = passed_along(sent, "chan", -1)
    refs = remodulate(sent, next_symbols)
    halo = from_behind(refs[:, length - LANES :], "tm", 1)
    owner_chan = incidence // owned
    slot = (owner_chan - chan_index) % chan_count * owned + incidence % owned
    slot_rows = jnp.broadcast_to(
        slot.T.reshape(PER_RECV * recv_count, 1), (PER_RECV * recv_count, LANES)
    )
    lag = jnp.arange(LANES, dtype=jnp.int32)
    gain_rows = jnp.where(
        lag < DELAYS,
        gains[0].T.reshape(PER_RECV * recv_count, 1),
        gains[1].T.reshape(PER_RECV * recv_count, 1),
    )
    gain_taps = jnp.where(
        delays.T.reshape(PER_RECV * recv_count, 1) == (lag & (DELAYS - 1)), gain_rows, 0.0
    )
    tap_high = lax.reduce_precision(gain_taps, 8, 7)
    tap_low = (gain_taps - tap_high).astype(jnp.bfloat16)
    gain_rows = jnp.concatenate([tap_high.astype(jnp.bfloat16), tap_low], axis=0)
    laid = lay_gains(gain_rows, slot_rows)
    received, parts, shifted = receive(
        slot, laid, refs, halo, echoes.reshape(2 * recv_count, length)
    )
    share = recv_count // tm_count
    corr_share = 256 * LANES // tm_count
    parts = jnp.sum(lax.all_to_all(parts, "tm", 0, 0, tiled=True), axis=0, keepdims=True)
    my_cross = parts[:, : PER_RECV * LANES]
    my_corr = jnp.broadcast_to(parts[:, PER_RECV * LANES :], (tm_count, corr_share))
    corr = lax.all_to_all(my_corr, "tm", 0, 0, tiled=True).reshape(256, LANES)
    my_slot = lax.dynamic_slice_in_dim(slot, tm_index * share, share, 0).reshape(PER_RECV)
    mine = solve(my_slot, corr, my_cross, tm_count)
    solved = lax.all_to_all(mine, "tm", 0, 0, tiled=True)
    cancelled, weights = cancel(solved, slot_rows, shifted, received)
    return (cancelled.reshape(2, recv_count, length), weights)


def solution(mesh):
    in_specs = (
        P("chan", "tm"),
        P("chan", None),
        P("chan", None),
        P(None, "chan", None),
        P(None, "chan", "tm"),
    )
    out_specs = (P(None, "chan", "tm"), P(None, "chan", None))
    return jax.shard_map(local, mesh=mesh, in_specs=in_specs, out_specs=out_specs, check_vma=False)
```
